32 devices in a mesh: ri: 4 (over z), orb: 8 (over y, x, core).
Axes of the slice: x: 2, y: 2, z: 4, core: 2. Of those that a mesh axis runs over, the one named last changes fastest.
Arguments:
- integrals: bfloat16 [2048, 8, 3072], P(('ri', 'orb')), may hold values from -0.41992188 to 0.41992188
- screen: int32 [8, 3, 128], P(None, None, ('ri', 'orb')), may hold values 0 or 1
- green_occ: bfloat16 [8, 3, 32, 32], replicated, may hold values from -0.625 to 0.625
- green_virt: bfloat16 [8, 32, 32], replicated, may hold values from -1 to 1
Outputs:
- chi: float32 [2048, 2048], P('ri', 'orb')
The draws below stay inside these ranges and needn't reach their ends.
All inputs are finite; a program needn't handle non-finite values. No bound on the sum of `screen` on one device may be relied on, other than what follows from the above.
Results may differ from the reference program's by a relative error of at most 0.0041.
Values may be sent and summed in bfloat16 or wider, within the bound.
No kernel may reach another device: no remote copies, remote signals or barrier semaphores. Data moves between devices by JAX's collectives and lax.ppermute only.
A program may use at most 256 MiB of HBM per device.

```python
import jax
import jax.numpy as jnp
from jax import lax

BF = 32
RB = 16
NG = 8
NPF = 2048
NPB = 128


def set_ends(values, own_key, smallest, largest):
    place = [jax.random.randint(jax.random.fold_in(own_key, axis), (), 0, length) for axis, length in enumerate(values.shape)]
    widest = values.shape.index(max(values.shape))
    next_to = place[:widest] + [(place[widest] + 1) % values.shape[widest]] + place[widest + 1:]
    return values.at[tuple(place)].set(smallest).at[tuple(next_to)].set(largest)


def levels(key, extent, pieces, smallest, largest):
    factor_of = 1.0
    for axis_at, parts in pieces:
        draws = jax.random.uniform(jax.random.fold_in(jax.random.fold_in(key, 6), axis_at), (parts,), jnp.float32, smallest / len(pieces), largest / len(pieces))
        factor_of = factor_of * jnp.repeat(jnp.exp(draws), extent[axis_at] // parts).reshape((-1,) + (1,) * (len(extent) - 1 - axis_at))
    return factor_of


def bell_draw(stream_key, dims, scale, reach, shards=(), kind=jnp.bfloat16):
    entries = jax.random.normal(stream_key, dims, jnp.float32) * scale
    if len(shards) > 0:
        entries = levels(stream_key, dims, shards, -0.22, 0.18) * entries
    return jnp.clip(entries, min=-reach, max=reach).astype(kind)


def setup_inputs(seed: int = 0) -> dict:
    splits = jax.random.split(jax.random.key(seed), 5)
    return {
        "integrals": bell_draw(splits[0], (NPF, NG, 3 * BF * BF), 0.07, 0.41992188, ((0, 32),)),
        "screen": set_ends((jax.random.randint(splits[1], (NG, 3, NPB), 0, 4) < 3).astype(jnp.int32), jax.random.fold_in(splits[1], 1), 0, 1),
        "green_occ": bell_draw(splits[2], (NG, 3, BF, BF), (3 * BF) ** -0.5, 0.625),
        "green_virt": bell_draw(splits[3], (NG, BF, BF), BF ** -0.5, 1.0),
    }


def green_apply(extended, green_occ, green_ext):
    groups = green_occ.shape[0]
    total = None
    for t in range(3):
        slab = extended[t:t + groups]
        padded = jnp.pad(slab, ((0, 0), (0, 0), (1, 1), (0, 0), (0, 0)))
        window = padded[:, :, 2 - t:5 - t]
        term = jnp.einsum("gnm,gmslp->gnslp", green_occ[:, t].astype(jnp.float32), window.astype(jnp.float32))
        total = term if total is None else total + term
    occ_side = total.astype(jnp.bfloat16)
    chosen = jnp.stack([green_ext[s:s + groups] for s in range(3)], axis=1)
    both = jnp.einsum("gnslp,gsla->gnsap", occ_side.astype(jnp.float32), chosen.astype(jnp.float32))
    return both.astype(jnp.bfloat16)


def reference(integrals, screen, green_occ, green_virt):
    rows = integrals.shape[0]
    groups = integrals.shape[1]
    unpacked = jnp.transpose(integrals.reshape(rows, groups, BF, 3, BF), (1, 2, 3, 4, 0))
    blocks = jnp.repeat(screen, RB, axis=2)
    target = jnp.arange(groups)[:, None] + jnp.arange(3)[None, :] - 1
    inside = ((target >= 0) & (target < groups)).astype(jnp.int32)
    keep = (blocks * inside[:, :, None]).astype(jnp.bfloat16)
    masked = unpacked * keep[:, None, :, None, :]
    extended = jnp.pad(masked, ((1, 1), (0, 0), (0, 0), (0, 0), (0, 0)))
    green_ext = jnp.pad(green_virt, ((1, 1), (0, 0), (0, 0)))
    both = green_apply(extended, green_occ, green_ext)
    width = both.shape[-1]
    return lax.dot_general(both.reshape(-1, width), masked.reshape(-1, width), (((0,), (0,)), ((), ())), preferred_element_type=jnp.float32)
```

```python
import functools

import jax
import jax.numpy as jnp
from jax import lax
from jax.experimental import pallas as pl
from jax.experimental.pallas import tpu as pltpu
from jax.sharding import PartitionSpec as P

RB = 16
CHUNKS = 2
BF16 = jnp.bfloat16
F32 = jnp.float32
VMEM = pl.BlockSpec(memory_space=pltpu.VMEM)
SMEM = pl.BlockSpec(memory_space=pltpu.SMEM)
LIMIT = 48 * 1024 * 1024


def iota(shape, dim):
    return lax.broadcasted_iota(jnp.int32, shape, dim)


def dot(x, y):
    return lax.dot_general(x, y, (((1,), (0,)), ((), ())), preferred_element_type=F32)


def dot_t(x, y):
    return lax.dot_general(x, y, (((1,), (1,)), ((), ())), preferred_element_type=F32)


def ones_where(test):
    return jnp.where(test, 1.0, 0.0).astype(BF16)


def cost(flops, moved):
    return pl.CostEstimate(flops=int(flops), bytes_accessed=int(moved), transcendentals=0)


def prep_kernel(groups, blocks, first, screen_ref, x_ref, out_ref, lanes_ref):
    rows = x_ref.shape[0]
    per = rows // groups
    lane, row = iota((1536, 128), 1), iota((1536, 128), 0)
    base = row - (lane // 8) * 96 - lane % 8
    for g in range(12):
        lanes_ref[:, g * 128 : (g + 1) * 128] = ones_where(base == g * 8)
    to, of = iota((rows, rows), 0), iota((rows, rows), 1)
    by_group = ones_where(of == (to % per) * groups + to // per)
    for h in range(2):
        x = dot(by_group, x_ref[:, h * 1536 : (h + 1) * 1536]).astype(BF16)
        for s in range(3):
            y = dot(x, lanes_ref[:, s * 512 : (s + 1) * 512])
            for a in range(groups):
                d = a + s - 1
                if not 0 <= d < groups:
                    continue
                for b in range(per // RB):
                    keep = screen_ref[(a * 3 + s) * blocks + first + b].astype(F32)
                    at = a * per + b * RB
                    z = (y[at : at + RB] * keep).astype(BF16)
                    for j in range(4):
                        col = (2 - s) * 1024 + j * 256 + h * 128
                        out_ref[d, b * RB : (b + 1) * RB, col : col + 128] = z[:, j * 128 : (j + 1) * 128]
    zeros = jnp.zeros((per, 1024), BF16)
    out_ref[0, :, :1024] = zeros
    out_ref[groups - 1, :, 2048:] = zeros


def prep(c, x, screen, groups, per):
    blocks = screen.shape[0] // (groups * 3)
    rows = per * groups
    return pl.pallas_call(
        functools.partial(prep_kernel, groups, blocks, c * (per // RB)),
        grid=(1,),
        out_shape=jax.ShapeDtypeStruct((groups, per, 3072), BF16),
        in_specs=[SMEM, pl.BlockSpec((rows, 3072), lambda i: (c, 0))],
        out_specs=pl.BlockSpec((groups, per, 3072), lambda i: (0, 0, 0)),
        scratch_shapes=[pltpu.VMEM((1536, 1536), BF16)],
        compiler_params=pltpu.CompilerParams(vmem_limit_bytes=LIMIT),
        cost_estimate=cost(4 * rows * 1536 * 1536, rows * 3072 * 4),
        name=f"prep{c}",
    )(screen, x)


def weights_kernel(d_ref, occ_ref, virt_ref, w1_ref, w2_ref):
    d = d_ref[0]
    last = occ_ref.shape[0] - 1
    spread = ones_where(iota((256, 32), 0) // 8 == iota((256, 32), 1))
    same = iota((256, 256), 0) % 8 == iota((256, 256), 1) % 8
    for c in range(3):
        at = jnp.clip(d + (c - 1), 0, last)
        for a in range(3):
            t = a - c + 1
            if 0 <= t <= 2:
                half = dot_t(spread, occ_ref[at, t]).astype(BF16)
                block = jnp.where(same, dot_t(half, spread), 0.0)
            else:
                block = jnp.zeros((256, 256), F32)
            w1_ref[a * 256 : (a + 1) * 256, c * 256 : (c + 1) * 256] = block.astype(BF16)
    row = iota((512, 32), 0)
    spread = ones_where((row // 128) * 8 + row % 8 == iota((512, 32), 1))
    same = (iota((512, 512), 0) % 128) // 8 == (iota((512, 512), 1) % 128) // 8
    half = dot(spread, virt_ref[d]).astype(BF16)
    w2_ref[...] = jnp.where(same, dot_t(half, spread), 0.0).astype(BF16)


def weights(d, occ, virt):
    return pl.pallas_call(
        weights_kernel,
        out_shape=(jax.ShapeDtypeStruct((768, 768), BF16), jax.ShapeDtypeStruct((512, 512), BF16)),
        in_specs=[SMEM, VMEM, VMEM],
        out_specs=(VMEM, VMEM),
        compiler_params=pltpu.CompilerParams(vmem_limit_bytes=LIMIT),
        cost_estimate=cost(1e8, 2e6),
        name="weights",
    )(d, occ, virt)


def apply_green(m_ref, w1_ref, w2_ref, y_ref, out_ref):
    for j in range(4):
        for c in range(3):
            lo, hi = max(c - 1, 0), min(c + 1, 2) + 1
            x = jnp.concatenate([m_ref[:, a * 1024 + j * 256 : a * 1024 + (j + 1) * 256] for a in range(lo, hi)], axis=1)
            y = dot(x, w1_ref[lo * 256 : hi * 256, c * 256 : (c + 1) * 256])
            y_ref[:, j * 768 + c * 256 : j * 768 + (c + 1) * 256] = y.astype(BF16)
    for c in range(3):
        for h in range(2):
            at = c * 256 + h * 128
            x = jnp.concatenate([y_ref[:, j * 768 + at : j * 768 + at + 128] for j in range(4)], axis=1)
            z = dot(x, w2_ref[...]).astype(BF16)
            for j in range(4):
                col = c * 1024 + j * 256 + h * 128
                out_ref[:, col : col + 128] = z[:, j * 128 : (j + 1) * 128]


def green_kernel(m_ref, w1_ref, w2_ref, out_ref, y_ref):
    apply_green(m_ref, w1_ref, w2_ref, y_ref, out_ref)


def green(m, w1, w2):
    rows = m.shape[0]
    return pl.pallas_call(
        green_kernel,
        out_shape=jax.ShapeDtypeStruct(m.shape, BF16),
        in_specs=[VMEM] * 3,
        out_specs=VMEM,
        scratch_shapes=[pltpu.VMEM((rows, 3072), BF16)],
        compiler_params=pltpu.CompilerParams(vmem_limit_bytes=LIMIT),
        cost_estimate=cost(rows * 7e6, rows * 3072 * 4),
        name="green",
    )(m, w1, w2)


def own_kernel(chunks, *refs):
    m_ref, out_ref = refs[chunks], refs[chunks + 1]
    rows = m_ref.shape[0]
    for i in range(chunks):
        out_ref[i * rows : (i + 1) * rows] = dot_t(refs[i][...], m_ref[...]).astype(BF16)


def own(bs, m):
    chunks, rows = len(bs), m.shape[0]
    return pl.pallas_call(
        functools.partial(own_kernel, chunks),
        out_shape=jax.ShapeDtypeStruct((chunks * rows, rows), BF16),
        in_specs=[VMEM] * (chunks + 1),
        out_specs=VMEM,
        compiler_params=pltpu.CompilerParams(vmem_limit_bytes=LIMIT),
        cost_estimate=cost(2 * chunks * rows * rows * 3072, (chunks + 1) * rows * 3072 * 2),
        name="own",
    )(*bs, m)


def pair_kernel(chunks, on_ref, m_ref, w1_ref, w2_ref, *refs):
    ms, bs = refs[:chunks], refs[chunks : 2 * chunks]
    mine_ref, theirs_ref, y_ref, b_ref = refs[2 * chunks :]
    rows = m_ref.shape[0]

    @pl.when(on_ref[0] > 0)
    def _():
        for i in range(chunks):
            mine_ref[i * rows : (i + 1) * rows] = dot_t(bs[i][...], m_ref[...]).astype(BF16)
        apply_green(m_ref, w1_ref, w2_ref, y_ref, b_ref)
        for i in range(chunks):
            theirs_ref[:, i * rows : (i + 1) * rows] = dot_t(b_ref[...], ms[i][...]).astype(BF16)

    @pl.when(on_ref[0] <= 0)
    def _():
        mine_ref[...] = jnp.zeros(mine_ref.shape, BF16)
        theirs_ref[...] = jnp.zeros(theirs_ref.shape, BF16)


def pair(on, m, w1, w2, ms, bs):
    chunks, rows = len(ms), m.shape[0]
    return pl.pallas_call(
        functools.partial(pair_kernel, chunks),
        out_shape=(
            jax.ShapeDtypeStruct((chunks * rows, rows), BF16),
            jax.ShapeDtypeStruct((rows, chunks * rows), BF16),
        ),
        in_specs=[SMEM] + [VMEM] * (3 + 2 * chunks),
        out_specs=(VMEM, VMEM),
        scratch_shapes=[pltpu.VMEM((rows, 3072), BF16)] * 2,
        compiler_params=pltpu.CompilerParams(vmem_limit_bytes=LIMIT),
        cost_estimate=cost(rows * 7e6 + 4 * chunks * rows * rows * 3072, (5 * rows) * 3072 * 2),
        name="pair",
    )(on, m, w1, w2, *ms, *bs)


def total_kernel(chunks, per, x_ref, out_ref):
    sources, rows, cols = x_ref.shape
    orbs = rows // (chunks * per)
    pieces = cols // (chunks * per)
    lane = iota((per, cols), 1) // per
    for c in range(chunks):
        for o in range(orbs):
            at = (c * orbs + o) * per
            total = x_ref[0, at : at + per].astype(F32)
            for k in range(1, sources):
                total = total + x_ref[k, at : at + per].astype(F32)
            moved = total
            for shift in sorted({(p * chunks + i) - (i * pieces + p) for p in range(pieces) for i in range(chunks)}):
                if shift == 0:
                    continue
                rolled = pltpu.roll(total, (shift * per) % cols, 1)
                came = (lane % chunks) * pieces + lane // chunks
                moved = jnp.where(lane - came == shift, rolled, moved)
            to = (o * chunks + c) * per
            out_ref[to : to + per] = moved


def total(x, chunks, per):
    return pl.pallas_call(
        functools.partial(total_kernel, chunks, per),
        out_shape=jax.ShapeDtypeStruct(x.shape[1:], F32),
        in_specs=[VMEM],
        out_specs=VMEM,
        compiler_params=pltpu.CompilerParams(vmem_limit_bytes=LIMIT),
        cost_estimate=cost(x.size, x.size * 2),
        name="total",
    )(x)


def local(planes, orbs, integrals, screen, green_occ, green_virt):
    rows, groups, _ = integrals.shape
    per = rows // CHUNKS
    half = planes // 2
    r = lax.axis_index("ri")
    o = lax.axis_index("orb")
    odd = o % 2
    p = jnp.where(odd == 1, planes - 1 - r, r)

    def send(x, pairs):
        if not pairs:
            return None
        flat = []
        for orb in range(orbs):
            for source, target in pairs:
                if orb % 2:
                    source, target = planes - 1 - source, planes - 1 - target
                flat.append((source * orbs + orb, target * orbs + orb))
        return lax.ppermute(x, ("ri", "orb"), flat)

    x = integrals.reshape(rows * groups, 3072)
    screen = screen.reshape(-1)
    w1, w2 = weights(jnp.reshape(o, (1,)).astype(jnp.int32), green_occ, green_virt)

    ms = []
    for c in range(CHUNKS):
        m = prep(c, x, screen, groups, per)
        m = lax.all_to_all(m, "orb", split_axis=0, concat_axis=0, tiled=True)
        ms.append(m.reshape(orbs * per, 3072))

    ahead = {s: [(q - 1, q) for q in range(s, min(planes - 1, half - 1 + s) + 1)] for s in range(1, planes)}
    behind = {s: [(q + 1, q) for q in range(half, planes - s)] for s in range(1, planes - half)}
    got = {}
    for c in range(CHUNKS):
        for s in ahead:
            got["f", s, c] = send(ms[c] if s == 1 else got["f", s - 1, c], ahead[s])
        for s in behind:
            got["b", s, c] = send(ms[c] if s == 1 else got["b", s - 1, c], behind[s])

    bs = [green(m, w1, w2) for m in ms]
    mine = {}
    back = {}
    for c in range(CHUNKS):
        mine[0, c] = own(bs, ms[c])
        for s in ahead:
            on = (p >= s) & (p <= min(planes - 1, half - 1 + s))
            mine["f", s, c], theirs = pair(jnp.reshape(on, (1,)).astype(jnp.int32), got["f", s, c], w1, w2, ms, bs)
            back["f", s, c] = send(theirs, [(q, q - s) for _, q in ahead[s]])
        for s in behind:
            on = (p >= half) & (p < planes - s)
            mine["b", s, c], theirs = pair(jnp.reshape(on, (1,)).astype(jnp.int32), got["b", s, c], w1, w2, ms, bs)
            back["b", s, c] = send(theirs, [(q, q + s) for _, q in behind[s]])

    def by_columns(kind, s):
        return jnp.concatenate([mine[kind, s, c] if kind else mine[0, c] for c in range(CHUNKS)], axis=1)

    def by_rows(kind, s):
        return jnp.concatenate([back[kind, s, c] for c in range(CHUNKS)], axis=0)

    shares = orbs // planes
    size = orbs * rows
    width = size // shares

    def shape_mine(x):
        return x.reshape(size, CHUNKS, shares, width // CHUNKS)

    blocks = []
    for q in range(-(planes - 1), planes):
        s = abs(q)
        if q == 0:
            block = by_columns(None, 0)
        else:
            lower, upper = None, None
            if q < 0:
                lower = by_columns("f", s)
                if s in behind:
                    upper = by_rows("b", s)
                block = lower if upper is None else jnp.where(p - s >= half, upper, lower)
            else:
                lower = by_rows("f", s)
                if s in behind:
                    upper = by_columns("b", s)
                block = lower if upper is None else jnp.where(p >= half, upper, lower)
        blocks.append(block)
    stack = jnp.stack([jnp.where(odd == 1, blocks[-1 - i], blocks[i]) for i in range(len(blocks))])
    chosen = lax.dynamic_slice_in_dim(stack, planes - 1 - r, planes, 0)
    chosen = chosen.reshape(planes, size, CHUNKS, shares, width // CHUNKS)
    chosen = jnp.transpose(chosen, (0, 3, 1, 2, 4)).reshape(orbs, size, width)
    parts = lax.all_to_all(chosen, "orb", split_axis=0, concat_axis=0, tiled=True)
    return total(parts, CHUNKS, per)


def solution(mesh):
    planes, orbs = mesh.shape["ri"], mesh.shape["orb"]
    placed = (P(("ri", "orb"), None, None), P(None, None, ("ri", "orb")), P(), P())
    return jax.shard_map(
        functools.partial(local, planes, orbs),
        mesh=mesh,
        in_specs=placed,
        out_specs=P("ri", "orb"),
        check_vma=False,
    )
```

```python
import functools

import jax
import jax.numpy as jnp
from jax import lax
from jax.experimental import pallas as pl
from jax.experimental.pallas import tpu as pltpu
from jax.sharding import PartitionSpec as P

RB = 16
CHUNKS = 2
BF16 = jnp.bfloat16
F32 = jnp.float32
VMEM = pl.BlockSpec(memory_space=pltpu.VMEM)
SMEM = pl.BlockSpec(memory_space=pltpu.SMEM)
MIB = 1024 * 1024


def iota(shape, dim):
    return lax.broadcasted_iota(jnp.int32, shape, dim)


def dot(x, y):
    return lax.dot_general(x, y, (((1,), (0,)), ((), ())), preferred_element_type=F32)


def dot_t(x, y):
    return lax.dot_general(x, y, (((1,), (1,)), ((), ())), preferred_element_type=F32)


def ones_where(test):
    return jnp.where(test, 1.0, 0.0).astype(BF16)


def cost(flops, moved):
    return pl.CostEstimate(flops=int(flops), bytes_accessed=int(moved), transcendentals=0)


def prep_kernel(groups, blocks, first, screen_ref, x_ref, out_ref, lanes_ref):
    rows = x_ref.shape[0]
    per = rows // groups
    lane, row = iota((1536, 128), 1), iota((1536, 128), 0)
    base = row - (lane // 8) * 96 - lane % 8
    for g in range(12):
        lanes_ref[:, g * 128 : (g + 1) * 128] = ones_where(base == g * 8)
    to, of = iota((rows, rows), 0), iota((rows, rows), 1)
    by_group = ones_where(of == (to % per) * groups + to // per)
    for h in range(2):
        x = dot(by_group, x_ref[:, h * 1536 : (h + 1) * 1536]).astype(BF16)
        for s in range(3):
            y = dot(x, lanes_ref[:, s * 512 : (s + 1) * 512])
            for a in range(groups):
                d = a + s - 1
                if not 0 <= d < groups:
                    continue
                for b in range(per // RB):
                    keep = screen_ref[(a * 3 + s) * blocks + first + b].astype(F32)
                    at = a * per + b * RB
                    z = (y[at : at + RB] * keep).astype(BF16)
                    for j in range(4):
                        col = (2 - s) * 1024 + j * 256 + h * 128
                        out_ref[d, b * RB : (b + 1) * RB, col : col + 128] = z[:, j * 128 : (j + 1) * 128]
    zeros = jnp.zeros((per, 1024), BF16)
    out_ref[0, :, :1024] = zeros
    out_ref[groups - 1, :, 2048:] = zeros


def prep(c, x, screen, groups, per):
    blocks = screen.shape[0] // (groups * 3)
    rows = per * groups
    return pl.pallas_call(
        functools.partial(prep_kernel, groups, blocks, c * (per // RB)),
        grid=(1,),
        out_shape=jax.ShapeDtypeStruct((groups, per, 3072), BF16),
        in_specs=[SMEM, pl.BlockSpec((rows, 3072), lambda i: (c, 0))],
        out_specs=pl.BlockSpec((groups, per, 3072), lambda i: (0, 0, 0)),
        scratch_shapes=[pltpu.VMEM((1536, 1536), BF16)],
        compiler_params=pltpu.CompilerParams(vmem_limit_bytes=24 * MIB),
        cost_estimate=cost(4 * rows * 1536 * 1536, rows * 3072 * 4),
    )(screen, x)


def weights_kernel(d_ref, occ_ref, virt_ref, w1_ref, w2_ref):
    d = d_ref[0]
    last = occ_ref.shape[0] - 1
    spread = ones_where(iota((256, 32), 0) // 8 == iota((256, 32), 1))
    same = iota((256, 256), 0) % 8 == iota((256, 256), 1) % 8
    for c in range(3):
        at = jnp.clip(d + (c - 1), 0, last)
        for a in range(3):
            t = a - c + 1
            if 0 <= t <= 2:
                half = dot_t(spread, occ_ref[at, t]).astype(BF16)
                block = jnp.where(same, dot_t(half, spread), 0.0)
            else:
                block = jnp.zeros((256, 256), F32)
            w1_ref[a * 256 : (a + 1) * 256, c * 256 : (c + 1) * 256] = block.astype(BF16)
    row = iota((512, 32), 0)
    spread = ones_where((row // 128) * 8 + row % 8 == iota((512, 32), 1))
    same = (iota((512, 512), 0) % 128) // 8 == (iota((512, 512), 1) % 128) // 8
    half = dot(spread, virt_ref[d]).astype(BF16)
    w2_ref[...] = jnp.where(same, dot_t(half, spread), 0.0).astype(BF16)


def weights(d, occ, virt):
    return pl.pallas_call(
        weights_kernel,
        out_shape=(jax.ShapeDtypeStruct((768, 768), BF16), jax.ShapeDtypeStruct((512, 512), BF16)),
        in_specs=[SMEM, VMEM, VMEM],
        out_specs=(VMEM, VMEM),
        compiler_params=pltpu.CompilerParams(vmem_limit_bytes=12 * MIB),
        cost_estimate=cost(1e8, 2e6),
        name="weights",
    )(d, occ, virt)


def apply_green(m_ref, w1_ref, w2_ref, y_ref, out_ref):
    for j in range(4):
        for c in range(3):
            lo, hi = max(c - 1, 0), min(c + 1, 2) + 1
            x = jnp.concatenate([m_ref[:, a * 1024 + j * 256 : a * 1024 + (j + 1) * 256] for a in range(lo, hi)], axis=1)
            y = dot(x, w1_ref[lo * 256 : hi * 256, c * 256 : (c + 1) * 256])
            y_ref[:, j * 768 + c * 256 : j * 768 + (c + 1) * 256] = y.astype(BF16)
    for c in range(3):
        for h in range(2):
            at = c * 256 + h * 128
            x = jnp.concatenate([y_ref[:, j * 768 + at : j * 768 + at + 128] for j in range(4)], axis=1)
            z = dot(x, w2_ref[...]).astype(BF16)
            for j in range(4):
                col = c * 1024 + j * 256 + h * 128
                out_ref[:, col : col + 128] = z[:, j * 128 : (j + 1) * 128]


def green_kernel(m_ref, w1_ref, w2_ref, out_ref, y_ref):
    apply_green(m_ref, w1_ref, w2_ref, y_ref, out_ref)


def green(m, w1, w2):
    rows = m.shape[0]
    return pl.pallas_call(
        green_kernel,
        out_shape=jax.ShapeDtypeStruct(m.shape, BF16),
        in_specs=[VMEM] * 3,
        out_specs=VMEM,
        scratch_shapes=[pltpu.VMEM((rows, 3072), BF16)],
        compiler_params=pltpu.CompilerParams(vmem_limit_bytes=12 * MIB),
        cost_estimate=cost(rows * 7e6, rows * 3072 * 4),
        name="green",
    )(m, w1, w2)


def own_kernel(b0_ref, b1_ref, m_ref, out_ref):
    for i, b_ref in enumerate((b0_ref, b1_ref)):
        x = dot_t(b_ref[...], m_ref[...]).astype(BF16)
        for h in range(2):
            width = out_ref.shape[3]
            out_ref[h, i] = x[:, h * width : (h + 1) * width]


def own(bs, m):
    rows = m.shape[0]
    return pl.pallas_call(
        own_kernel,
        out_shape=jax.ShapeDtypeStruct((2, 2, rows, rows // 2), BF16),
        in_specs=[VMEM] * 3,
        out_specs=VMEM,
        compiler_params=pltpu.CompilerParams(vmem_limit_bytes=12 * MIB),
        cost_estimate=cost(4 * rows * rows * 3072, 3 * rows * 3072 * 2),
        name="own",
    )(*bs, m)


def ahead_here(s, p, planes):
    return (p >= s) & (p <= min(planes - 1, planes // 2 - 1 + s))


def behind_here(s, p, planes):
    return (p >= planes // 2) & (p < planes - s)


def has_behind(s, planes):
    return 1 <= planes - s < planes - planes // 2


def pair_kernel(planes, s, where_ref, m_ref, *refs):
    p = where_ref[0] // 2
    both = has_behind(s, planes)
    far_ref = refs[0] if both else None
    w1_ref, w2_ref, m0_ref, m1_ref, b0_ref, b1_ref, mine_ref, theirs_ref, y_ref, b_ref = refs[both : both + 10]
    width = mine_ref.shape[3]
    ahead = ahead_here(s, p, planes)
    on = ahead
    if both:
        behind = behind_here(planes - s, p, planes)
        on = ahead | behind
        held_ref = refs[-1]

        @pl.when(ahead)
        def _():
            held_ref[...] = m_ref[...]

        @pl.when(behind)
        def _():
            held_ref[...] = far_ref[...]
    else:
        held_ref = m_ref

    @pl.when(on)
    def _():
        for i, own_ref in enumerate((b0_ref, b1_ref)):
            x = dot_t(own_ref[...], held_ref[...]).astype(BF16)
            for h in range(2):
                mine_ref[h, i] = x[:, h * width : (h + 1) * width]
        apply_green(held_ref, w1_ref, w2_ref, y_ref, b_ref)
        for i, own_ref in enumerate((m0_ref, m1_ref)):
            x = dot_t(b_ref[...], own_ref[...]).astype(BF16)
            for h in range(2):
                theirs_ref[h, i] = x[:, h * width : (h + 1) * width]


def pair(planes, s, where, held, w1, w2, ms, bs):
    rows = ms[0].shape[0]
    block = jax.ShapeDtypeStruct((2, 2, rows, rows // 2), BF16)
    return pl.pallas_call(
        functools.partial(pair_kernel, planes, s),
        out_shape=(block, block),
        in_specs=[SMEM] + [VMEM] * (6 + len(held)),
        out_specs=(VMEM, VMEM),
        scratch_shapes=[pltpu.VMEM((rows, 3072), BF16)] * (1 + len(held)),
        compiler_params=pltpu.CompilerParams(vmem_limit_bytes=20 * MIB),
        cost_estimate=cost(rows * 7e6 + 8 * rows * rows * 3072, 5 * rows * 3072 * 2),
    )(where, *held, w1, w2, *ms, *bs)


def select_kernel(planes, keys, where_ref, *refs):
    out_ref = refs[-1]
    half = planes // 2
    p, odd = where_ref[0] // 2, where_ref[0] % 2
    for (side, s), x_ref in zip(keys, refs[:-1], strict=True):
        if side == "own":
            used, at = None, p
        elif side == "mine":
            used, at = ahead_here(s, p, planes), p - s
        else:
            used, at = (p + s < planes) & (p < half), p + s
        if side != "own" and has_behind(s, planes):
            t = planes - s
            if side == "mine":
                other, far = behind_here(t, p, planes), p + t
            else:
                other, far = p - t >= half, p - t
            at = jnp.where(used, at, far)
            used = used | other
        at = jnp.where(odd == 1, planes - 1 - at, at)

        def copy(x_ref=x_ref, at=at):
            out_ref[at] = x_ref[...]

        if used is None:
            copy()
        else:
            pl.when(used)(copy)


def select(planes, where, parts):
    keys, arrays = list(parts), list(parts.values())
    return pl.pallas_call(
        functools.partial(select_kernel, planes, keys),
        out_shape=jax.ShapeDtypeStruct((planes,) + arrays[0].shape, BF16),
        in_specs=[SMEM] + [VMEM] * len(arrays),
        out_specs=VMEM,
        compiler_params=pltpu.CompilerParams(vmem_limit_bytes=12 * MIB),
        cost_estimate=cost(1e5, 4 * planes * arrays[0].size),
        name="select",
    )(where, *arrays)


def total_kernel(planes, per, here_ref, x0_ref, x1_ref, out_ref):
    orbs, _, rows, width = x0_ref.shape
    half = planes // 2
    r, q = here_ref[0] // planes, here_ref[0] % planes
    straight = []
    for odd in range(2):
        p, t = (planes - 1 - r, planes - 1 - q) if odd else (r, q)
        straight.append((p == t) | ((t < p) & (t < half)) | ((t > p) & (p >= half)))
    blocks = width // per
    lane = iota((per, width), 1) // per
    for o in range(rows // per):
        at = slice(o * per, (o + 1) * per)

        def sums(x_ref, i, first, step, at=at):
            x = x_ref[first, i, at].astype(F32)
            for k in range(first + step, orbs, step):
                x = x + x_ref[k, i, at].astype(F32)
            return x

        quads = {(0, 0): sums(x0_ref, 0, 0, 1), (1, 1): sums(x1_ref, 1, 0, 1)}
        low, high = 0.0, 0.0
        for odd in range(2):
            a, b = sums(x0_ref, 1, odd, 2), sums(x1_ref, 0, odd, 2)
            low = low + jnp.where(straight[odd], a, b)
            high = high + jnp.where(straight[odd], b, a)
        quads[1, 0], quads[0, 1] = low, high
        for i in range(2):
            for tile in range(2):
                moved = None
                for b in range(blocks):
                    came = blocks // 2 * tile + b // 2
                    shift = ((b - came) * per) % width
                    x = quads[i, b % 2]
                    x = pltpu.roll(x, shift, 1) if shift else x
                    moved = x if moved is None else jnp.where(lane == b, x, moved)
                to = (o * 2 + i) * per
                out_ref[to : to + per, tile * width : (tile + 1) * width] = moved


def total(planes, per, here, parts):
    _, _, rows, width = parts[0].shape
    return pl.pallas_call(
        functools.partial(total_kernel, planes, per),
        out_shape=jax.ShapeDtypeStruct((2 * rows, 2 * width), F32),
        in_specs=[SMEM, VMEM, VMEM],
        out_specs=VMEM,
        compiler_params=pltpu.CompilerParams(vmem_limit_bytes=12 * MIB),
        cost_estimate=cost(1e7, 4 * parts[0].size),
        name="total",
    )(here, *parts)


def hops(planes):
    half = planes // 2
    ahead = {("f", s): [(q - 1, q) for q in range(s, min(planes - 1, half - 1 + s) + 1)] for s in range(1, planes)}
    behind = {("b", s): [(q + 1, q) for q in range(half, planes - s)] for s in range(1, planes - half)}
    return {k: v for k, v in (ahead | behind).items() if v}


def local(planes, orbs, integrals, screen, green_occ, green_virt):
    rows, groups, _ = integrals.shape
    per = rows // CHUNKS
    r = lax.axis_index("ri")
    o = lax.axis_index("orb")
    odd = o % 2
    p = jnp.where(odd == 1, planes - 1 - r, r)
    where = jnp.reshape(p * 2 + odd, (1,)).astype(jnp.int32)
    shares = orbs // planes
    here = jnp.reshape(r * planes + o // shares, (1,)).astype(jnp.int32)

    def send(x, pairs):
        flat = []
        for orb in range(orbs):
            for source, target in pairs:
                if orb % 2:
                    source, target = planes - 1 - source, planes - 1 - target
                flat.append((source * orbs + orb, target * orbs + orb))
        return lax.ppermute(x, ("ri", "orb"), flat)

    def swap(x):
        return lax.all_to_all(x, "orb", split_axis=0, concat_axis=0, tiled=True)

    x = integrals.reshape(rows * groups, 3072)
    screen = screen.reshape(-1)
    w1, w2 = weights(jnp.reshape(o, (1,)).astype(jnp.int32), green_occ, green_virt)
    ms, bs = [], []
    for c in range(CHUNKS):
        m = prep(c, x, screen, groups, per)
        ms.append(swap(m).reshape(orbs * per, 3072))
        bs.append(green(ms[c], w1, w2))

    steps = hops(planes)
    got, parts = {}, [{}, {}]
    for c in range(CHUNKS):
        for kind, s in steps:
            held = ms[c] if s == 1 else got[kind, s - 1, c]
            got[kind, s, c] = send(held, steps[kind, s])
    for c in range(CHUNKS):
        parts[c]["own", 0] = own(bs, ms[c])
        for s in range(1, planes):
            held = [got["f", s, c]]
            pairs = [(t, t - s) for _, t in steps["f", s]]
            if has_behind(s, planes):
                held.append(got["b", planes - s, c])
                pairs += [(t, t + planes - s) for _, t in steps["b", planes - s]]
            mine, theirs = pair(planes, s, where, held, w1, w2, ms, bs)
            parts[c]["mine", s] = mine
            parts[c]["theirs", s] = send(theirs, pairs)
    sums = []
    for c in range(CHUNKS):
        block = select(planes, where, parts[c])
        block = block.reshape((orbs,) + block.shape[2:])
        sums.append(swap(block))
    return total(planes, per, here, sums)


def solution(mesh):
    planes, orbs = mesh.shape["ri"], mesh.shape["orb"]
    placed = (P(("ri", "orb"), None, None), P(None, None, ("ri", "orb")), P(), P())

    def body(*args):
        return local(planes, orbs, *args)

    return jax.shard_map(body, mesh=mesh, in_specs=placed, out_specs=P("ri", "orb"), check_vma=False)
```

```python
import functools

import jax
import jax.numpy as jnp
from jax import lax
from jax.experimental import pallas as pl
from jax.experimental.pallas import tpu as pltpu
from jax.sharding import PartitionSpec as P

RB = 16
CHUNKS = 2
BF16 = jnp.bfloat16
F32 = jnp.float32
VMEM = pl.BlockSpec(memory_space=pltpu.VMEM)
SMEM = pl.BlockSpec(memory_space=pltpu.SMEM)
MIB = 1024 * 1024


def iota(shape, dim):
    return lax.broadcasted_iota(jnp.int32, shape, dim)


def dot(x, y):
    return lax.dot_general(x, y, (((1,), (0,)), ((), ())), preferred_element_type=F32)


def dot_t(x, y):
    return lax.dot_general(x, y, (((1,), (1,)), ((), ())), preferred_element_type=F32)


def ones_where(test):
    return jnp.where(test, 1.0, 0.0).astype(BF16)


def cost(flops, moved):
    return pl.CostEstimate(flops=int(flops), bytes_accessed=int(moved), transcendentals=0)


def prep_kernel(groups, blocks, c, per, screen_ref, x_ref, out_ref, lanes_ref):
    rows, first = per * groups, c * (per // RB)
    lane, row = iota((1536, 128), 1), iota((1536, 128), 0)
    base = row - (lane // 8) * 96 - lane % 8
    for g in range(12):
        lanes_ref[:, g * 128 : (g + 1) * 128] = ones_where(base == g * 8)
    to, of = iota((rows, rows), 0), iota((rows, rows), 1)
    by_group = ones_where(of == (to % per) * groups + to // per)
    for h in range(2):
        x = dot(by_group, x_ref[:, h * 1536 : (h + 1) * 1536]).astype(BF16)
        for s in range(3):
            y = dot(x, lanes_ref[:, s * 512 : (s + 1) * 512])
            for a in range(groups):
                d = a + s - 1
                if not 0 <= d < groups:
                    continue
                for b in range(per // RB):
                    keep = screen_ref[(a * 3 + s) * blocks + first + b].astype(F32)
                    at = a * per + b * RB
                    z = (y[at : at + RB] * keep).astype(BF16)
                    for j in range(4):
                        col = (2 - s) * 1024 + j * 256 + h * 128
                        out_ref[d, b * RB : (b + 1) * RB, col : col + 128] = z[:, j * 128 : (j + 1) * 128]
    zeros = jnp.zeros((per, 1024), BF16)
    out_ref[0, :, :1024] = zeros
    out_ref[groups - 1, :, 2048:] = zeros


def prep(c, x, screen, groups, per):
    blocks = screen.shape[0] // (groups * 3)
    rows = per * groups
    return pl.pallas_call(
        functools.partial(prep_kernel, groups, blocks, c, per),
        out_shape=jax.ShapeDtypeStruct((groups, per, 3072), BF16),
        in_specs=[SMEM, VMEM],
        out_specs=VMEM,
        scratch_shapes=[pltpu.VMEM((1536, 1536), BF16)],
        compiler_params=pltpu.CompilerParams(vmem_limit_bytes=24 * MIB),
        cost_estimate=cost(4 * rows * 1536 * 1536, rows * 3072 * 4),
    )(screen, x[c * rows : (c + 1) * rows])


def weights_kernel(occ_ref, virt_ref, w1_ref, w2_ref):
    d = lax.axis_index("orb")
    last = occ_ref.shape[0] - 1
    spread = ones_where(iota((256, 32), 0) // 8 == iota((256, 32), 1))
    same = iota((256, 256), 0) % 8 == iota((256, 256), 1) % 8
    for c in range(3):
        at = jnp.clip(d + (c - 1), 0, last)
        for a in range(3):
            t = a - c + 1
            if 0 <= t <= 2:
                half = dot_t(spread, occ_ref[at, t]).astype(BF16)
                block = jnp.where(same, dot_t(half, spread), 0.0)
            else:
                block = jnp.zeros((256, 256), F32)
            w1_ref[a * 256 : (a + 1) * 256, c * 256 : (c + 1) * 256] = block.astype(BF16)
    row = iota((512, 32), 0)
    spread = ones_where((row // 128) * 8 + row % 8 == iota((512, 32), 1))
    same = (iota((512, 512), 0) % 128) // 8 == (iota((512, 512), 1) % 128) // 8
    half = dot(spread, virt_ref[d]).astype(BF16)
    w2_ref[...] = jnp.where(same, dot_t(half, spread), 0.0).astype(BF16)


def weights(occ, virt):
    return pl.pallas_call(
        weights_kernel,
        out_shape=(jax.ShapeDtypeStruct((768, 768), BF16), jax.ShapeDtypeStruct((512, 512), BF16)),
        in_specs=[VMEM, VMEM],
        out_specs=(VMEM, VMEM),
        compiler_params=pltpu.CompilerParams(vmem_limit_bytes=12 * MIB),
        cost_estimate=cost(1e8, 2e6),
        name="weights",
    )(occ, virt)


def apply_green(m_ref, w1_ref, w2_ref, y_ref, out_ref):
    for j in range(4):
        for c in range(3):
            lo, hi = max(c - 1, 0), min(c + 1, 2) + 1
            x = jnp.concatenate([m_ref[:, a * 1024 + j * 256 : a * 1024 + (j + 1) * 256] for a in range(lo, hi)], axis=1)
            y = dot(x, w1_ref[lo * 256 : hi * 256, c * 256 : (c + 1) * 256])
            y_ref[:, j * 768 + c * 256 : j * 768 + (c + 1) * 256] = y.astype(BF16)
    for c in range(3):
        for h in range(2):
            at = c * 256 + h * 128
            x = jnp.concatenate([y_ref[:, j * 768 + at : j * 768 + at + 128] for j in range(4)], axis=1)
            z = dot(x, w2_ref[...]).astype(BF16)
            for j in range(4):
                col = c * 1024 + j * 256 + h * 128
                out_ref[:, col : col + 128] = z[:, j * 128 : (j + 1) * 128]


def green_kernel(m_ref, w1_ref, w2_ref, out_ref, y_ref):
    apply_green(m_ref, w1_ref, w2_ref, y_ref, out_ref)


def green(m, w1, w2):
    rows = m.shape[0]
    return pl.pallas_call(
        green_kernel,
        out_shape=jax.ShapeDtypeStruct(m.shape, BF16),
        in_specs=[VMEM] * 3,
        out_specs=VMEM,
        scratch_shapes=[pltpu.VMEM((rows, 3072), BF16)],
        compiler_params=pltpu.CompilerParams(vmem_limit_bytes=12 * MIB),
        cost_estimate=cost(rows * 7e6, rows * 3072 * 4),
        name="green",
    )(m, w1, w2)


def own_kernel(b0_ref, b1_ref, m_ref, out_ref):
    for i, b_ref in enumerate((b0_ref, b1_ref)):
        x = dot_t(b_ref[...], m_ref[...]).astype(BF16)
        for h in range(2):
            width = out_ref.shape[3]
            out_ref[h, i] = x[:, h * width : (h + 1) * width]


def own(bs, m):
    rows = m.shape[0]
    return pl.pallas_call(
        own_kernel,
        out_shape=jax.ShapeDtypeStruct((2, 2, rows, rows // 2), BF16),
        in_specs=[VMEM] * 3,
        out_specs=VMEM,
        compiler_params=pltpu.CompilerParams(vmem_limit_bytes=12 * MIB),
        cost_estimate=cost(4 * rows * rows * 3072, 3 * rows * 3072 * 2),
        name="own",
    )(*bs, m)


USERS = {"f1": (1, 2), "f2": (2, 3), "g": (2, 2)}


def place():
    r, odd = lax.axis_index("ri"), lax.axis_index("orb") % 2
    return jnp.where(odd == 1, 3 - r, r), odd


def products(left0_ref, left1_ref, right_ref, out_ref):
    width = out_ref.shape[3]
    for i, x_ref in enumerate((left0_ref, left1_ref)):
        x = dot_t(x_ref[...], right_ref[...]).astype(BF16)
        for h in range(2):
            out_ref[h, i] = x[:, h * width : (h + 1) * width]


def products_t(left_ref, right0_ref, right1_ref, out_ref):
    width = out_ref.shape[3]
    for i, x_ref in enumerate((right0_ref, right1_ref)):
        x = dot_t(left_ref[...], x_ref[...]).astype(BF16)
        for h in range(2):
            out_ref[h, i] = x[:, h * width : (h + 1) * width]


def pair_kernel(kind, m_ref, w1_ref, w2_ref, m0_ref, m1_ref, b0_ref, b1_ref, mine_ref, theirs_ref, b_ref, y_ref):
    p, _ = place()
    first, last = USERS[kind]

    @pl.when((p >= first) & (p <= last))
    def _():
        apply_green(m_ref, w1_ref, w2_ref, y_ref, b_ref)
        products_t(b_ref, m0_ref, m1_ref, theirs_ref)
        products(b0_ref, b1_ref, m_ref, mine_ref)


def pair(kind, m, w1, w2, ms, bs):
    rows = m.shape[0]
    block = jax.ShapeDtypeStruct((2, 2, rows, rows // 2), BF16)
    return pl.pallas_call(
        functools.partial(pair_kernel, kind),
        out_shape=(block, block, jax.ShapeDtypeStruct(m.shape, BF16)),
        in_specs=[VMEM] * 7,
        out_specs=(VMEM,) * 3,
        scratch_shapes=[pltpu.VMEM((rows, 3072), BF16)],
        compiler_params=pltpu.CompilerParams(vmem_limit_bytes=12 * MIB),
        cost_estimate=cost(rows * 7e6 + 8 * rows * rows * 3072, 5 * rows * 3072 * 2),
    )(m, w1, w2, *ms, *bs)


def cross_kernel(m_ref, b_ref, m0_ref, m1_ref, b0_ref, b1_ref, held_ref, up_ref, down_ref):
    @pl.when(place()[0] == 2)
    def _():
        products_t(b_ref, m0_ref, m1_ref, down_ref)
        products(b0_ref, b1_ref, m_ref, up_ref.at[1])
        up_ref[0] = held_ref[...]


def cross(m, b, ms, bs, held):
    rows = m.shape[0]
    return pl.pallas_call(
        cross_kernel,
        out_shape=(jax.ShapeDtypeStruct((2,) + held.shape, BF16), jax.ShapeDtypeStruct(held.shape, BF16)),
        in_specs=[VMEM] * 7,
        out_specs=(VMEM,) * 2,
        compiler_params=pltpu.CompilerParams(vmem_limit_bytes=12 * MIB),
        cost_estimate=cost(8 * rows * rows * 3072, 5 * rows * 3072 * 2),
        name="cross",
    )(m, b, *ms, *bs, held)


def select_kernel(own_ref, m1_ref, m2_ref, mg_ref, t1_ref, t2_ref, up_ref, down_ref, *refs):
    outs, all_ref = refs[:-1], refs[-1]
    p, odd = place()
    me = lax.axis_index("orb")

    def put(used, at, x_ref, *index):
        @pl.when(used)
        def _():
            q = jnp.where(odd == 1, 3 - at, at)
            for h in range(2):
                all_ref[(q * 2 + h) ^ me] = x_ref[(*index, h)]

    put(p >= 0, p, own_ref)
    put((p == 1) | (p == 2), p - 1, m1_ref)
    put(p >= 2, p - 2, m2_ref)
    put(p == 2, 3, mg_ref)
    put(p <= 1, p + 1, t1_ref)
    put(p <= 1, p + 2, t2_ref)
    put(p == 3, 2, up_ref, 0)
    put(p == 3, 0, up_ref, 1)
    put(p == 0, 3, down_ref)
    for k, out_ref in enumerate(outs):
        out_ref[...] = all_ref[k]


def select(parts):
    shape = (2,) + parts[0].shape[2:]
    return pl.pallas_call(
        select_kernel,
        out_shape=(jax.ShapeDtypeStruct(shape, BF16),) * 8,
        in_specs=[VMEM] * len(parts),
        out_specs=(VMEM,) * 8,
        scratch_shapes=[pltpu.VMEM((8,) + shape, BF16)],
        compiler_params=pltpu.CompilerParams(vmem_limit_bytes=12 * MIB),
        cost_estimate=cost(1e5, 16 * parts[0].size),
        name="select",
    )(*parts)


def total_kernel(per, *refs):
    x0, x1, out_ref = refs[:8], refs[8:16], refs[16]
    _, rows, width = x0[0].shape
    me = lax.axis_index("orb")
    r, q = lax.axis_index("ri"), me // 2
    straight = []
    for other in range(2):
        odd = (me + other) % 2
        p, t = jnp.where(odd == 1, 3 - r, r), jnp.where(odd == 1, 3 - q, q)
        straight.append((p == t) | ((t < p) & (t < 2)) | ((t > p) & (p >= 2)))
    blocks = width // per
    lane = iota((per, width), 1) // per
    for o in range(rows // per):
        at = slice(o * per, (o + 1) * per)

        def sums(xs, i, at=at):
            x = xs[0][i, at].astype(F32)
            for x_ref in xs[1:]:
                x = x + x_ref[i, at].astype(F32)
            return x

        quads = {(0, 0): sums(x0, 0), (1, 1): sums(x1, 1)}
        low, high = 0.0, 0.0
        for other in range(2):
            a, b = sums(x0[other::2], 1), sums(x1[other::2], 0)
            low = low + jnp.where(straight[other], a, b)
            high = high + jnp.where(straight[other], b, a)
        quads[1, 0], quads[0, 1] = low, high
        for i in range(2):
            for tile in range(2):
                moved = None
                for b in range(blocks):
                    came = blocks // 2 * tile + b // 2
                    shift = ((b - came) * per) % width
                    x = quads[i, b % 2]
                    x = pltpu.roll(x, shift, 1) if shift else x
                    moved = x if moved is None else jnp.where(lane == b, x, moved)
                to = (o * 2 + i) * per
                out_ref[to : to + per, tile * width : (tile + 1) * width] = moved


def total(per, parts):
    _, rows, width = parts[0].shape
    return pl.pallas_call(
        functools.partial(total_kernel, per),
        out_shape=jax.ShapeDtypeStruct((2 * rows, 2 * width), F32),
        in_specs=[VMEM] * len(parts),
        out_specs=VMEM,
        compiler_params=pltpu.CompilerParams(vmem_limit_bytes=12 * MIB),
        cost_estimate=cost(1e7, 4 * parts[0].size),
        name="total",
    )(*parts)


def local(planes, orbs, integrals, screen, green_occ, green_virt):
    rows, groups, _ = integrals.shape
    per = rows // CHUNKS

    def send(x, pairs):
        flat = []
        for orb in range(orbs):
            for source, target in pairs:
                if orb % 2:
                    source, target = planes - 1 - source, planes - 1 - target
                flat.append((source * orbs + orb, target * orbs + orb))
        return lax.ppermute(x, ("ri", "orb"), flat)

    def swap(x):
        return lax.all_to_all(x, "orb", split_axis=0, concat_axis=0, tiled=True)

    x = integrals.reshape(rows * groups, 3072)
    screen = screen.reshape(-1)
    w1, w2 = weights(green_occ, green_virt)
    ms, bs = [], []
    for c in range(CHUNKS):
        m = prep(c, x, screen, groups, per)
        ms.append(swap(m).reshape(orbs * per, 3072))
        bs.append(green(ms[c], w1, w2))

    mine, theirs, b_of, got = {}, {}, {}, {}
    for c in range(CHUNKS):
        got["f1", c] = send(ms[c], [(0, 1), (1, 2)])
        got["f2", c] = send(got["f1", c], [(1, 2), (2, 3)])
        got["g", c] = send(ms[c], [(3, 2)])
        for kind in USERS:
            mine[kind, c], theirs[kind, c], b_of[kind, c] = pair(kind, got[kind, c], w1, w2, ms, bs)
    sums = []
    for c in range(CHUNKS):
        own_block = own(bs, ms[c])
        far = [[x["g", i] for i in range(CHUNKS)] for x in (got, b_of)]
        up, down = cross(got["f2", c], b_of["f2", c], *far, theirs["g", c])
        back = [
            send(theirs["f1", c], [(1, 0), (2, 1)]),
            send(theirs["f2", c], [(2, 0), (3, 1)]),
            send(up, [(2, 3)]),
            send(down, [(2, 0)]),
        ]
        pieces = select([own_block] + [mine[kind, c] for kind in USERS] + back)
        sums.append(pieces[0])
        for k in range(1, orbs):
            pairs = [(q * orbs + i, q * orbs + (i ^ k)) for q in range(planes) for i in range(orbs)]
            sums.append(lax.ppermute(pieces[k], ("ri", "orb"), pairs))
    return total(per, sums)


def padded_2(block, sides, width):
    for axis, dim in sides:
        count = lax.axis_size(axis)
        forward = [(i, i + 1) for i in range(count - 1)]
        backward = [(target, source) for source, target in forward]
        low = lax.ppermute(
            lax.slice_in_dim(block, block.shape[dim] - width, None, axis=dim), axis, forward
        )
        high = lax.ppermute(lax.slice_in_dim(block, 0, width, axis=dim), axis, backward)
        block = jnp.concatenate([low, block, high], axis=dim)
    return block


def green_apply(extended, green_occ, green_ext):
    groups = green_occ.shape[0]
    rows = extended.shape[0]
    basis = green_occ.shape[-1]
    shaped = extended.reshape(rows, groups + 2, basis, 3, basis)
    total = None
    for t in range(3):
        slab = shaped[:, t : t + groups]
        padded = jnp.pad(slab, ((0, 0), (0, 0), (0, 0), (1, 1), (0, 0)))
        window = padded[:, :, :, 2 - t : 5 - t]
        term = jnp.einsum(
            "gnm,pgmsl->pgnsl", green_occ[:, t], window, preferred_element_type=jnp.float32
        )
        total = term if total is None else total + term
    occ_side = total.astype(jnp.bfloat16)
    chosen = jnp.stack([green_ext[s : s + groups] for s in range(3)], axis=1)
    both = jnp.einsum("pgnsl,gsla->pgnsa", occ_side, chosen, preferred_element_type=jnp.float32)
    return both.astype(jnp.bfloat16).reshape(rows, groups, -1)


def local_any(integrals, screen, green_occ, green_virt):
    rows = integrals.shape[0]
    groups = integrals.shape[1]
    basis = green_occ.shape[-1]
    blocks = jnp.repeat(screen, RB, axis=2)
    target = jnp.arange(groups)[:, None] + jnp.arange(3)[None, :] - 1
    inside = ((target >= 0) & (target < groups)).astype(jnp.int32)
    keep = jnp.transpose(blocks * inside[:, :, None], (2, 0, 1)).astype(jnp.bfloat16)
    shaped = integrals.reshape(rows, groups, basis, 3, basis)
    masked = (shaped * keep[:, :, None, :, None]).reshape(rows, groups, -1)
    green_ext = jnp.pad(green_virt, ((1, 1), (0, 0), (0, 0)))
    masked_mine = lax.all_to_all(masked, "orb", split_axis=1, concat_axis=0, tiled=True)
    local_groups = masked_mine.shape[1]
    first = lax.axis_index("orb") * local_groups
    extended = padded_2(masked_mine, (("orb", 1),), 1)
    occ_mine = lax.dynamic_slice_in_dim(green_occ, first, local_groups, 0)
    virt_mine = lax.dynamic_slice_in_dim(green_ext, first, local_groups + 2, 0)
    both_mine = green_apply(extended, occ_mine, virt_mine)
    left = both_mine.reshape(both_mine.shape[0], -1)
    piece = lax.all_gather(masked_mine, "ri", axis=0, tiled=True)
    right = piece.reshape(piece.shape[0], -1)
    partial_chi = lax.dot_general(
        left, right, (((1,), (1,)), ((), ())), preferred_element_type=jnp.float32
    )
    return lax.psum_scatter(partial_chi, "orb", scatter_dimension=1, tiled=True)


def solution(mesh):
    planes, orbs = mesh.shape["ri"], mesh.shape["orb"]
    placed = (P(("ri", "orb"), None, None), P(None, None, ("ri", "orb")), P(), P())

    if planes != 4 or orbs != 8:
        return jax.shard_map(local_any, mesh=mesh, in_specs=placed, out_specs=P("ri", "orb"), check_vma=False)

    def body(*args):
        return local(planes, orbs, *args)

    return jax.shard_map(body, mesh=mesh, in_specs=placed, out_specs=P("ri", "orb"), check_vma=False)
```

```python
import functools

import jax
import jax.numpy as jnp
from jax import lax
from jax.experimental import pallas as pl
from jax.experimental.pallas import tpu as pltpu
from jax.sharding import PartitionSpec as P

RB = 16
CHUNKS = 2
BF16 = jnp.bfloat16
F32 = jnp.float32
VMEM = pl.BlockSpec(memory_space=pltpu.VMEM)
SMEM = pl.BlockSpec(memory_space=pltpu.SMEM)
MIB = 1024 * 1024


def iota(shape, dim):
    return lax.broadcasted_iota(jnp.int32, shape, dim)


def dot(x, y):
    return lax.dot_general(x, y, (((1,), (0,)), ((), ())), preferred_element_type=F32)


def dot_t(x, y):
    return lax.dot_general(x, y, (((1,), (1,)), ((), ())), preferred_element_type=F32)


def ones_where(test):
    return jnp.where(test, 1.0, 0.0).astype(BF16)


def cost(flops, moved):
    return pl.CostEstimate(flops=int(flops), bytes_accessed=int(moved), transcendentals=0)


def prep_kernel(groups, blocks, c, per, screen_ref, x_ref, out_ref, *refs):
    lanes_ref = refs[-1]
    rows, first = per * groups, c * (per // RB)
    lane, row = iota((1536, 128), 1), iota((1536, 128), 0)
    base = row - (lane // 8) * 96 - lane % 8
    for g in range(12):
        lanes_ref[:, g * 128 : (g + 1) * 128] = ones_where(base == g * 8)
    to, of = iota((rows, rows), 0), iota((rows, rows), 1)
    by_group = ones_where(of == (to % per) * groups + to // per)
    for h in range(2):
        x = dot(by_group, x_ref[:, h * 1536 : (h + 1) * 1536]).astype(BF16)
        for s in range(3):
            y = dot(x, lanes_ref[:, s * 512 : (s + 1) * 512])
            for a in range(groups):
                d = a + s - 1
                if not 0 <= d < groups:
                    continue
                for b in range(per // RB):
                    keep = screen_ref[(a * 3 + s) * blocks + first + b].astype(F32)
                    at = a * per + b * RB
                    z = (y[at : at + RB] * keep).astype(BF16)
                    for j in range(4):
                        col = (2 - s) * 1024 + j * 256 + h * 128
                        out_ref[d, b * RB : (b + 1) * RB, col : col + 128] = z[:, j * 128 : (j + 1) * 128]
    zeros = jnp.zeros((per, 1024), BF16)
    out_ref[0, :, :1024] = zeros
    out_ref[groups - 1, :, 2048:] = zeros
    for odd, half_ref in enumerate(refs[:-1]):
        for k in range(groups // 2):
            half_ref[k] = out_ref[2 * k + odd]


def prep(c, x, screen, groups, per, halves):
    blocks = screen.shape[0] // (groups * 3)
    rows = per * groups
    shapes = [jax.ShapeDtypeStruct((groups, per, 3072), BF16)]
    shapes += [jax.ShapeDtypeStruct((groups // 2, per, 3072), BF16)] * (2 * halves)
    return pl.pallas_call(
        functools.partial(prep_kernel, groups, blocks, c, per),
        out_shape=shapes,
        in_specs=[SMEM, VMEM],
        out_specs=[VMEM] * len(shapes),
        scratch_shapes=[pltpu.VMEM((1536, 1536), BF16)],
        compiler_params=pltpu.CompilerParams(vmem_limit_bytes=24 * MIB),
        cost_estimate=cost(4 * rows * 1536 * 1536, rows * 3072 * 4),
    )(screen, x[c * rows : (c + 1) * rows])


def unpack_kernel(even_ref, odd_ref, *outs):
    me = lax.axis_index("orb")
    for k, out_ref in enumerate(outs):
        to = me ^ k
        for odd, x_ref in enumerate((even_ref, odd_ref)):

            @pl.when(to % 2 == odd)
            def _(x_ref=x_ref, out_ref=out_ref, to=to):
                out_ref[...] = x_ref[to // 2]


def unpack(even, odd):
    return pl.pallas_call(
        unpack_kernel,
        out_shape=[jax.ShapeDtypeStruct(even.shape[1:], BF16)] * 8,
        in_specs=[VMEM] * 2,
        out_specs=[VMEM] * 8,
        compiler_params=pltpu.CompilerParams(vmem_limit_bytes=12 * MIB),
        cost_estimate=cost(1e5, 8 * even.size),
        name="unpack",
    )(even, odd)


def assemble_kernel(*refs):
    out_ref = refs[-1]
    per = refs[0].shape[0]
    me = lax.axis_index("orb")
    for k, x_ref in enumerate(refs[:-1]):
        out_ref[pl.ds(pl.multiple_of((me ^ k) * per, per), per)] = x_ref[...]


def assemble(pieces):
    per, width = pieces[0].shape
    return pl.pallas_call(
        assemble_kernel,
        out_shape=jax.ShapeDtypeStruct((8 * per, width), BF16),
        in_specs=[VMEM] * 8,
        out_specs=VMEM,
        compiler_params=pltpu.CompilerParams(vmem_limit_bytes=12 * MIB),
        cost_estimate=cost(1e5, 32 * per * width),
        name="assemble",
    )(*pieces)


def weights_kernel(occ_ref, virt_ref, w1_ref, w2_ref):
    d = lax.axis_index("orb")
    last = occ_ref.shape[0] - 1
    spread = ones_where(iota((256, 32), 0) // 8 == iota((256, 32), 1))
    same = iota((256, 256), 0) % 8 == iota((256, 256), 1) % 8
    for c in range(3):
        at = jnp.clip(d + (c - 1), 0, last)
        for a in range(3):
            t = a - c + 1
            if 0 <= t <= 2:
                half = dot_t(spread, occ_ref[at, t]).astype(BF16)
                block = jnp.where(same, dot_t(half, spread), 0.0)
            else:
                block = jnp.zeros((256, 256), F32)
            w1_ref[a * 256 : (a + 1) * 256, c * 256 : (c + 1) * 256] = block.astype(BF16)
    row = iota((512, 32), 0)
    spread = ones_where((row // 128) * 8 + row % 8 == iota((512, 32), 1))
    same = (iota((512, 512), 0) % 128) // 8 == (iota((512, 512), 1) % 128) // 8
    half = dot(spread, virt_ref[d]).astype(BF16)
    w2_ref[...] = jnp.where(same, dot_t(half, spread), 0.0).astype(BF16)


def weights(occ, virt):
    return pl.pallas_call(
        weights_kernel,
        out_shape=(jax.ShapeDtypeStruct((768, 768), BF16), jax.ShapeDtypeStruct((512, 512), BF16)),
        in_specs=[VMEM, VMEM],
        out_specs=(VMEM, VMEM),
        compiler_params=pltpu.CompilerParams(vmem_limit_bytes=12 * MIB),
        cost_estimate=cost(1e8, 2e6),
        name="weights",
    )(occ, virt)


def apply_green(m_ref, w1_ref, w2_ref, y_ref, out_ref):
    for j in range(4):
        for c in range(3):
            lo, hi = max(c - 1, 0), min(c + 1, 2) + 1
            x = jnp.concatenate([m_ref[:, a * 1024 + j * 256 : a * 1024 + (j + 1) * 256] for a in range(lo, hi)], axis=1)
            y = dot(x, w1_ref[lo * 256 : hi * 256, c * 256 : (c + 1) * 256])
            y_ref[:, j * 768 + c * 256 : j * 768 + (c + 1) * 256] = y.astype(BF16)
    for c in range(3):
        for h in range(2):
            at = c * 256 + h * 128
            x = jnp.concatenate([y_ref[:, j * 768 + at : j * 768 + at + 128] for j in range(4)], axis=1)
            z = dot(x, w2_ref[...]).astype(BF16)
            for j in range(4):
                col = c * 1024 + j * 256 + h * 128
                out_ref[:, col : col + 128] = z[:, j * 128 : (j + 1) * 128]


def green_kernel(m0_ref, m1_ref, w1_ref, w2_ref, out_ref, kept_ref, y_ref):
    kept_ref[0] = m0_ref[...]
    kept_ref[1] = m1_ref[...]

    @pl.loop(0, 2)
    def _(c):
        apply_green(kept_ref.at[c], w1_ref, w2_ref, y_ref, out_ref.at[c])


def green(ms, w1, w2):
    rows = ms[0].shape[0]
    return pl.pallas_call(
        green_kernel,
        out_shape=(jax.ShapeDtypeStruct((2, rows, 3072), BF16),) * 2,
        in_specs=[VMEM] * 4,
        out_specs=(VMEM,) * 2,
        scratch_shapes=[pltpu.VMEM((rows, 3072), BF16)],
        compiler_params=pltpu.CompilerParams(vmem_limit_bytes=12 * MIB),
        cost_estimate=cost(rows * 14e6, rows * 3072 * 12),
        name="green",
    )(*ms, w1, w2)


def halves_to(x, out_ref, i):
    width = out_ref.shape[3]
    for h in range(2):
        out_ref[h, i] = x[:, h * width : (h + 1) * width].astype(BF16)


def own_kernel(c, b_ref, m_ref, out_ref):
    @pl.loop(0, 2)
    def _(i):
        halves_to(dot_t(b_ref[i], m_ref[c]), out_ref, i)


def own(b, m, c):
    rows = m.shape[1]
    return pl.pallas_call(
        functools.partial(own_kernel, c),
        out_shape=jax.ShapeDtypeStruct((2, 2, rows, rows // 2), BF16),
        in_specs=[VMEM] * 2,
        out_specs=VMEM,
        compiler_params=pltpu.CompilerParams(vmem_limit_bytes=12 * MIB),
        cost_estimate=cost(4 * rows * rows * 3072, 3 * rows * 3072 * 2),
        name="own",
    )(b, m)


USERS = {"f1": (1, 2), "f2": (2, 3), "g": (2, 2)}


def place():
    r, odd = lax.axis_index("ri"), lax.axis_index("orb") % 2
    return jnp.where(odd == 1, 3 - r, r), odd


def pair_kernel(kind, m_ref, w1_ref, w2_ref, kept_ref, green_ref, mine_ref, theirs_ref, b_ref, y_ref):
    p, _ = place()
    first, last = USERS[kind]

    @pl.when((p >= first) & (p <= last))
    def _():
        apply_green(m_ref, w1_ref, w2_ref, y_ref, b_ref)

        @pl.loop(0, 2)
        def _(i):
            halves_to(dot_t(b_ref[...], kept_ref[i]), theirs_ref, i)
            halves_to(dot_t(green_ref[i], m_ref[...]), mine_ref, i)


def pair(kind, m, w1, w2, kept, b):
    rows = m.shape[0]
    block = jax.ShapeDtypeStruct((2, 2, rows, rows // 2), BF16)
    return pl.pallas_call(
        functools.partial(pair_kernel, kind),
        out_shape=(block, block, jax.ShapeDtypeStruct(m.shape, BF16)),
        in_specs=[VMEM] * 5,
        out_specs=(VMEM,) * 3,
        scratch_shapes=[pltpu.VMEM((rows, 3072), BF16)],
        compiler_params=pltpu.CompilerParams(vmem_limit_bytes=12 * MIB),
        cost_estimate=cost(rows * 7e6 + 8 * rows * rows * 3072, 5 * rows * 3072 * 2),
    )(m, w1, w2, kept, b)


def cross_kernel(m_ref, b_ref, m0_ref, m1_ref, b0_ref, b1_ref, held_ref, up_ref, down_ref):
    @pl.when(place()[0] == 2)
    def _():
        for i, (far_m_ref, far_b_ref) in enumerate(((m0_ref, b0_ref), (m1_ref, b1_ref))):
            halves_to(dot_t(b_ref[...], far_m_ref[...]), down_ref, i)
            halves_to(dot_t(far_b_ref[...], m_ref[...]), up_ref.at[1], i)
        up_ref[0] = held_ref[...]


def cross(m, b, ms, bs, held):
    rows = m.shape[0]
    return pl.pallas_call(
        cross_kernel,
        out_shape=(jax.ShapeDtypeStruct((2,) + held.shape, BF16), jax.ShapeDtypeStruct(held.shape, BF16)),
        in_specs=[VMEM] * 7,
        out_specs=(VMEM,) * 2,
        compiler_params=pltpu.CompilerParams(vmem_limit_bytes=12 * MIB),
        cost_estimate=cost(8 * rows * rows * 3072, 5 * rows * 3072 * 2),
        name="cross",
    )(m, b, *ms, *bs, held)


def select_kernel(own_ref, m1_ref, m2_ref, mg_ref, t1_ref, t2_ref, up_ref, down_ref, *refs):
    outs, all_ref = refs[:-1], refs[-1]
    p, odd = place()
    me = lax.axis_index("orb")

    def put(used, at, x_ref, *index):
        @pl.when(used)
        def _():
            q = jnp.where(odd == 1, 3 - at, at)
            for h in range(2):
                all_ref[(q * 2 + h) ^ me] = x_ref[(*index, h)]

    put(p >= 0, p, own_ref)
    put((p == 1) | (p == 2), p - 1, m1_ref)
    put(p >= 2, p - 2, m2_ref)
    put(p == 2, 3, mg_ref)
    put(p <= 1, p + 1, t1_ref)
    put(p <= 1, p + 2, t2_ref)
    put(p == 3, 2, up_ref, 0)
    put(p == 3, 0, up_ref, 1)
    put(p == 0, 3, down_ref)
    for k, out_ref in enumerate(outs):
        out_ref[...] = all_ref[k]


def select(parts):
    shape = (2,) + parts[0].shape[2:]
    return pl.pallas_call(
        select_kernel,
        out_shape=(jax.ShapeDtypeStruct(shape, BF16),) * 8,
        in_specs=[VMEM] * len(parts),
        out_specs=(VMEM,) * 8,
        scratch_shapes=[pltpu.VMEM((8,) + shape, BF16)],
        compiler_params=pltpu.CompilerParams(vmem_limit_bytes=12 * MIB),
        cost_estimate=cost(1e5, 16 * parts[0].size),
        name="select",
    )(*parts)


def total_kernel(per, *refs):
    x0, x1, out_ref = refs[:8], refs[8:16], refs[16]
    _, rows, width = x0[0].shape
    me = lax.axis_index("orb")
    r, q = lax.axis_index("ri"), me // 2
    straight = []
    for other in range(2):
        odd = (me + other) % 2
        p, t = jnp.where(odd == 1, 3 - r, r), jnp.where(odd == 1, 3 - q, q)
        straight.append((p == t) | ((t < p) & (t < 2)) | ((t > p) & (p >= 2)))
    blocks = width // per
    lane = iota((per, width), 1) // per
    for o in range(rows // per):
        at = slice(o * per, (o + 1) * per)

        def sums(xs, i, at=at):
            x = xs[0][i, at].astype(F32)
            for x_ref in xs[1:]:
                x = x + x_ref[i, at].astype(F32)
            return x

        quads = {(0, 0): sums(x0, 0), (1, 1): sums(x1, 1)}
        low, high = 0.0, 0.0
        for other in range(2):
            a, b = sums(x0[other::2], 1), sums(x1[other::2], 0)
            low = low + jnp.where(straight[other], a, b)
            high = high + jnp.where(straight[other], b, a)
        quads[1, 0], quads[0, 1] = low, high
        for i in range(2):
            for tile in range(2):
                moved = None
                for b in range(blocks):
                    came = blocks // 2 * tile + b // 2
                    shift = ((b - came) * per) % width
                    x = quads[i, b % 2]
                    x = pltpu.roll(x, shift, 1) if shift else x
                    moved = x if moved is None else jnp.where(lane == b, x, moved)
                to = (o * 2 + i) * per
                out_ref[to : to + per, tile * width : (tile + 1) * width] = moved


def total(per, parts):
    _, rows, width = parts[0].shape
    return pl.pallas_call(
        functools.partial(total_kernel, per),
        out_shape=jax.ShapeDtypeStruct((2 * rows, 2 * width), F32),
        in_specs=[VMEM] * len(parts),
        out_specs=VMEM,
        compiler_params=pltpu.CompilerParams(vmem_limit_bytes=12 * MIB),
        cost_estimate=cost(1e7, 4 * parts[0].size),
        name="total",
    )(*parts)


def local(planes, orbs, integrals, screen, green_occ, green_virt):
    rows, groups, _ = integrals.shape
    per = rows // CHUNKS

    def send(x, pairs):
        flat = []
        for orb in range(orbs):
            for source, target in pairs:
                if orb % 2:
                    source, target = planes - 1 - source, planes - 1 - target
                flat.append((source * orbs + orb, target * orbs + orb))
        return lax.ppermute(x, ("ri", "orb"), flat)

    def swap(x):
        return lax.all_to_all(x, "orb", split_axis=0, concat_axis=0, tiled=True)

    x = integrals.reshape(rows * groups, 3072)
    screen = screen.reshape(-1)
    w1, w2 = weights(green_occ, green_virt)

    def xors(pieces):
        out = [pieces[0]]
        for k in range(1, orbs):
            pairs = [(q * orbs + i, q * orbs + (i ^ k)) for q in range(planes) for i in range(orbs)]
            out.append(lax.ppermute(pieces[k], ("ri", "orb"), pairs))
        return out

    ms = []
    for c in range(CHUNKS):
        m, *halves = prep(c, x, screen, groups, per, c > 0)
        ms.append(swap(m).reshape(orbs * per, 3072))
    b, kept = green(ms, w1, w2)
    even = lax.ppermute(halves[0], "ri", [(0, 1), (1, 2)])
    odd = lax.ppermute(halves[1], "ri", [(3, 2), (2, 1)])
    pieces = unpack(even, odd)
    pieces = xors(pieces)
    hopped = assemble(pieces)

    mine, theirs, b_of, got = {}, {}, {}, {}
    for c in range(CHUNKS):
        got["f1", c] = send(ms[c], [(0, 1), (1, 2)]) if c == 0 else hopped
        got["f2", c] = send(got["f1", c], [(1, 2), (2, 3)])
        got["g", c] = send(ms[c], [(3, 2)])
        for kind in USERS:
            mine[kind, c], theirs[kind, c], b_of[kind, c] = pair(kind, got[kind, c], w1, w2, kept, b)
    sums = []
    for c in range(CHUNKS):
        own_block = own(b, kept, c)
        far = [[x["g", i] for i in range(CHUNKS)] for x in (got, b_of)]
        up, down = cross(got["f2", c], b_of["f2", c], *far, theirs["g", c])
        back = [
            send(theirs["f1", c], [(1, 0), (2, 1)]),
            send(theirs["f2", c], [(2, 0), (3, 1)]),
            send(up, [(2, 3)]),
            send(down, [(2, 0)]),
        ]
        pieces = select([own_block] + [mine[kind, c] for kind in USERS] + back)
        sums += xors(pieces)
    return total(per, sums)


def padded_2(block, sides, width):
    for axis, dim in sides:
        count = lax.axis_size(axis)
        forward = [(i, i + 1) for i in range(count - 1)]
        backward = [(target, source) for source, target in forward]
        low = lax.ppermute(
            lax.slice_in_dim(block, block.shape[dim] - width, None, axis=dim), axis, forward
        )
        high = lax.ppermute(lax.slice_in_dim(block, 0, width, axis=dim), axis, backward)
        block = jnp.concatenate([low, block, high], axis=dim)
    return block


def green_apply(extended, green_occ, green_ext):
    groups = green_occ.shape[0]
    rows = extended.shape[0]
    basis = green_occ.shape[-1]
    shaped = extended.reshape(rows, groups + 2, basis, 3, basis)
    total = None
    for t in range(3):
        slab = shaped[:, t : t + groups]
        padded = jnp.pad(slab, ((0, 0), (0, 0), (0, 0), (1, 1), (0, 0)))
        window = padded[:, :, :, 2 - t : 5 - t]
        term = jnp.einsum(
            "gnm,pgmsl->pgnsl", green_occ[:, t], window, preferred_element_type=jnp.float32
        )
        total = term if total is None else total + term
    occ_side = total.astype(jnp.bfloat16)
    chosen = jnp.stack([green_ext[s : s + groups] for s in range(3)], axis=1)
    both = jnp.einsum("pgnsl,gsla->pgnsa", occ_side, chosen, preferred_element_type=jnp.float32)
    return both.astype(jnp.bfloat16).reshape(rows, groups, -1)


def local_any(integrals, screen, green_occ, green_virt):
    rows = integrals.shape[0]
    groups = integrals.shape[1]
    basis = green_occ.shape[-1]
    blocks = jnp.repeat(screen, RB, axis=2)
    target = jnp.arange(groups)[:, None] + jnp.arange(3)[None, :] - 1
    inside = ((target >= 0) & (target < groups)).astype(jnp.int32)
    keep = jnp.transpose(blocks * inside[:, :, None], (2, 0, 1)).astype(jnp.bfloat16)
    shaped = integrals.reshape(rows, groups, basis, 3, basis)
    masked = (shaped * keep[:, :, None, :, None]).reshape(rows, groups, -1)
    green_ext = jnp.pad(green_virt, ((1, 1), (0, 0), (0, 0)))
    masked_mine = lax.all_to_all(masked, "orb", split_axis=1, concat_axis=0, tiled=True)
    local_groups = masked_mine.shape[1]
    first = lax.axis_index("orb") * local_groups
    extended = padded_2(masked_mine, (("orb", 1),), 1)
    occ_mine = lax.dynamic_slice_in_dim(green_occ, first, local_groups, 0)
    virt_mine = lax.dynamic_slice_in_dim(green_ext, first, local_groups + 2, 0)
    both_mine = green_apply(extended, occ_mine, virt_mine)
    left = both_mine.reshape(both_mine.shape[0], -1)
    piece = lax.all_gather(masked_mine, "ri", axis=0, tiled=True)
    right = piece.reshape(piece.shape[0], -1)
    partial_chi = lax.dot_general(
        left, right, (((1,), (1,)), ((), ())), preferred_element_type=jnp.float32
    )
    return lax.psum_scatter(partial_chi, "orb", scatter_dimension=1, tiled=True)


def solution(mesh):
    planes, orbs = mesh.shape["ri"], mesh.shape["orb"]
    placed = (P(("ri", "orb"), None, None), P(None, None, ("ri", "orb")), P(), P())

    if planes != 4 or orbs != 8:
        return jax.shard_map(local_any, mesh=mesh, in_specs=placed, out_specs=P("ri", "orb"), check_vma=False)

    def body(*args):
        return local(planes, orbs, *args)

    return jax.shard_map(body, mesh=mesh, in_specs=placed, out_specs=P("ri", "orb"), check_vma=False)
```

```python
import functools

import jax
import jax.numpy as jnp
from jax import lax
from jax.experimental import pallas as pl
from jax.experimental.pallas import tpu as pltpu
from jax.sharding import PartitionSpec as P

RB = 16
CHUNKS = 2
BF16 = jnp.bfloat16
F32 = jnp.float32
VMEM = pl.BlockSpec(memory_space=pltpu.VMEM)
SMEM = pl.BlockSpec(memory_space=pltpu.SMEM)
MIB = 1024 * 1024


def iota(shape, dim):
    return lax.broadcasted_iota(jnp.int32, shape, dim)


def dot(x, y):
    return lax.dot_general(x, y, (((1,), (0,)), ((), ())), preferred_element_type=F32)


def dot_t(x, y):
    return lax.dot_general(x, y, (((1,), (1,)), ((), ())), preferred_element_type=F32)


def ones_where(test):
    return jnp.where(test, 1.0, 0.0).astype(BF16)


def cost(flops, moved):
    return pl.CostEstimate(flops=int(flops), bytes_accessed=int(moved), transcendentals=0)


def prep_kernel(groups, blocks, c, per, apart, screen_ref, x_ref, *refs):
    if apart:
        *outs, lanes_ref, out_ref = refs
    else:
        out_ref, lanes_ref = refs
    rows, first = per * groups, c * (per // RB)
    lane, row = iota((1536, 128), 1), iota((1536, 128), 0)
    base = row - (lane // 8) * 96 - lane % 8
    for g in range(12):
        lanes_ref[:, g * 128 : (g + 1) * 128] = ones_where(base == g * 8)
    to, of = iota((rows, rows), 0), iota((rows, rows), 1)
    by_group = ones_where(of == (to % per) * groups + to // per)
    for h in range(2):
        x = dot(by_group, x_ref[:, h * 1536 : (h + 1) * 1536]).astype(BF16)
        for s in range(3):
            y = dot(x, lanes_ref[:, s * 512 : (s + 1) * 512])
            for a in range(groups):
                d = a + s - 1
                if not 0 <= d < groups:
                    continue
                for b in range(per // RB):
                    keep = screen_ref[(a * 3 + s) * blocks + first + b].astype(F32)
                    at = a * per + b * RB
                    z = (y[at : at + RB] * keep).astype(BF16)
                    for j in range(4):
                        col = (2 - s) * 1024 + j * 256 + h * 128
                        out_ref[d, b * RB : (b + 1) * RB, col : col + 128] = z[:, j * 128 : (j + 1) * 128]
    zeros = jnp.zeros((per, 1024), BF16)
    out_ref[0, :, :1024] = zeros
    out_ref[groups - 1, :, 2048:] = zeros
    if apart:
        me = lax.axis_index("orb")
        for k in range(groups):
            outs[k][...] = out_ref[me ^ k]
        for odd, half_ref in enumerate(outs[groups:]):
            for k in range(groups // 2):
                half_ref[k] = out_ref[2 * k + odd]


def prep(c, x, screen, groups, per, apart):
    blocks = screen.shape[0] // (groups * 3)
    rows = per * groups
    shapes = [jax.ShapeDtypeStruct((groups, per, 3072), BF16)]
    scratch = [pltpu.VMEM((1536, 1536), BF16)]
    if apart:
        scratch.append(pltpu.VMEM((groups, per, 3072), BF16))
        shapes = [jax.ShapeDtypeStruct((per, 3072), BF16)] * groups
        shapes += [jax.ShapeDtypeStruct((groups // 2, per, 3072), BF16)] * 2
    return pl.pallas_call(
        functools.partial(prep_kernel, groups, blocks, c, per, apart),
        out_shape=shapes,
        in_specs=[SMEM, VMEM],
        out_specs=[VMEM] * len(shapes),
        scratch_shapes=scratch,
        compiler_params=pltpu.CompilerParams(vmem_limit_bytes=24 * MIB),
        cost_estimate=cost(4 * rows * 1536 * 1536, rows * 3072 * 4),
    )(screen, x[c * rows : (c + 1) * rows])


def unpack_kernel(even_ref, odd_ref, *outs):
    me = lax.axis_index("orb")
    for k, out_ref in enumerate(outs):
        to = me ^ k
        for odd, x_ref in enumerate((even_ref, odd_ref)):

            @pl.when(to % 2 == odd)
            def _(x_ref=x_ref, out_ref=out_ref, to=to):
                out_ref[...] = x_ref[to // 2]


def unpack(even, odd):
    return pl.pallas_call(
        unpack_kernel,
        out_shape=[jax.ShapeDtypeStruct(even.shape[1:], BF16)] * 8,
        in_specs=[VMEM] * 2,
        out_specs=[VMEM] * 8,
        compiler_params=pltpu.CompilerParams(vmem_limit_bytes=12 * MIB),
        cost_estimate=cost(1e5, 8 * even.size),
        name="unpack",
    )(even, odd)


def assemble_kernel(*refs):
    out_ref = refs[-1]
    per = refs[0].shape[0]
    me = lax.axis_index("orb")
    for k, x_ref in enumerate(refs[:-1]):
        out_ref[pl.ds(pl.multiple_of((me ^ k) * per, per), per)] = x_ref[...]


def assemble(pieces):
    per, width = pieces[0].shape
    return pl.pallas_call(
        assemble_kernel,
        out_shape=jax.ShapeDtypeStruct((8 * per, width), BF16),
        in_specs=[VMEM] * 8,
        out_specs=VMEM,
        compiler_params=pltpu.CompilerParams(vmem_limit_bytes=12 * MIB),
        cost_estimate=cost(1e5, 32 * per * width),
        name="assemble",
    )(*pieces)


def weights_kernel(occ_ref, virt_ref, w1_ref, w2_ref):
    d = lax.axis_index("orb")
    last = occ_ref.shape[0] - 1
    spread = ones_where(iota((256, 32), 0) // 8 == iota((256, 32), 1))
    same = iota((256, 256), 0) % 8 == iota((256, 256), 1) % 8
    for c in range(3):
        at = jnp.clip(d + (c - 1), 0, last)
        for a in range(3):
            t = a - c + 1
            if 0 <= t <= 2:
                half = dot_t(spread, occ_ref[at, t]).astype(BF16)
                block = jnp.where(same, dot_t(half, spread), 0.0)
            else:
                block = jnp.zeros((256, 256), F32)
            w1_ref[a * 256 : (a + 1) * 256, c * 256 : (c + 1) * 256] = block.astype(BF16)
    row = iota((512, 32), 0)
    spread = ones_where((row // 128) * 8 + row % 8 == iota((512, 32), 1))
    same = (iota((512, 512), 0) % 128) // 8 == (iota((512, 512), 1) % 128) // 8
    half = dot(spread, virt_ref[d]).astype(BF16)
    w2_ref[...] = jnp.where(same, dot_t(half, spread), 0.0).astype(BF16)


def weights(occ, virt):
    return pl.pallas_call(
        weights_kernel,
        out_shape=(jax.ShapeDtypeStruct((768, 768), BF16), jax.ShapeDtypeStruct((512, 512), BF16)),
        in_specs=[VMEM, VMEM],
        out_specs=(VMEM, VMEM),
        compiler_params=pltpu.CompilerParams(vmem_limit_bytes=12 * MIB),
        cost_estimate=cost(1e8, 2e6),
        name="weights",
    )(occ, virt)


def apply_green(m_ref, w1_ref, w2_ref, y_ref, out_ref):
    for j in range(4):
        for c in range(3):
            lo, hi = max(c - 1, 0), min(c + 1, 2) + 1
            x = jnp.concatenate([m_ref[:, a * 1024 + j * 256 : a * 1024 + (j + 1) * 256] for a in range(lo, hi)], axis=1)
            y = dot(x, w1_ref[lo * 256 : hi * 256, c * 256 : (c + 1) * 256])
            y_ref[:, j * 768 + c * 256 : j * 768 + (c + 1) * 256] = y.astype(BF16)
    for c in range(3):
        for h in range(2):
            at = c * 256 + h * 128
            x = jnp.concatenate([y_ref[:, j * 768 + at : j * 768 + at + 128] for j in range(4)], axis=1)
            z = dot(x, w2_ref[...]).astype(BF16)
            for j in range(4):
                col = c * 1024 + j * 256 + h * 128
                out_ref[:, col : col + 128] = z[:, j * 128 : (j + 1) * 128]


def green_kernel(far, m0_ref, m1_ref, w1_ref, w2_ref, out_ref, kept_ref, y_ref):
    def run():
        kept_ref[0] = m0_ref[...]
        kept_ref[1] = m1_ref[...]

        @pl.loop(0, 2)
        def _(c):
            apply_green(kept_ref.at[c], w1_ref, w2_ref, y_ref, out_ref.at[c])

    if far:
        pl.when(place()[0] == 2)(run)
    else:
        run()


def green(ms, w1, w2, far):
    rows = ms[0].shape[0]
    return pl.pallas_call(
        functools.partial(green_kernel, far),
        out_shape=(jax.ShapeDtypeStruct((2, rows, 3072), BF16),) * 2,
        in_specs=[VMEM] * 4,
        out_specs=(VMEM,) * 2,
        scratch_shapes=[pltpu.VMEM((rows, 3072), BF16)],
        compiler_params=pltpu.CompilerParams(vmem_limit_bytes=12 * MIB),
        cost_estimate=cost(rows * 14e6, rows * 3072 * 12),
        name="green",
    )(*ms, w1, w2)


def halves_to(x, out_ref, i):
    width = out_ref.shape[3]
    for h in range(2):
        out_ref[h, i] = x[:, h * width : (h + 1) * width].astype(BF16)


def own_kernel(c, b_ref, m_ref, out_ref):
    @pl.loop(0, 2)
    def _(i):
        halves_to(dot_t(b_ref[i], m_ref[c]), out_ref, i)


def own(b, m, c):
    rows = m.shape[1]
    return pl.pallas_call(
        functools.partial(own_kernel, c),
        out_shape=jax.ShapeDtypeStruct((2, 2, rows, rows // 2), BF16),
        in_specs=[VMEM] * 2,
        out_specs=VMEM,
        compiler_params=pltpu.CompilerParams(vmem_limit_bytes=12 * MIB),
        cost_estimate=cost(4 * rows * rows * 3072, 3 * rows * 3072 * 2),
        name="own",
    )(b, m)


USERS = {"f1": (1, 3), "f2": (2, 3)}


def place():
    r, odd = lax.axis_index("ri"), lax.axis_index("orb") % 2
    return jnp.where(odd == 1, 3 - r, r), odd


def pair_kernel(kind, m_ref, w1_ref, w2_ref, kept_ref, green_ref, mine_ref, theirs_ref, b_ref, y_ref):
    p, _ = place()
    first, last = USERS[kind]

    @pl.when((p >= first) & (p <= last))
    def _():
        apply_green(m_ref, w1_ref, w2_ref, y_ref, b_ref)

        @pl.loop(0, 2)
        def _(i):
            halves_to(dot_t(b_ref[...], kept_ref[i]), theirs_ref, i)
            halves_to(dot_t(green_ref[i], m_ref[...]), mine_ref, i)


def pair(kind, m, w1, w2, kept, b):
    rows = m.shape[0]
    keep = kind == "f2"
    block = jax.ShapeDtypeStruct((2, 2, rows, rows // 2), BF16)
    return pl.pallas_call(
        functools.partial(pair_kernel, kind),
        out_shape=(block, block) + (jax.ShapeDtypeStruct(m.shape, BF16),) * keep,
        in_specs=[VMEM] * 5,
        out_specs=(VMEM,) * (2 + keep),
        scratch_shapes=[pltpu.VMEM((rows, 3072), BF16)] * (2 - keep),
        compiler_params=pltpu.CompilerParams(vmem_limit_bytes=12 * MIB),
        cost_estimate=cost(rows * 7e6 + 8 * rows * rows * 3072, 5 * rows * 3072 * 2),
    )(m, w1, w2, kept, b)


def cross_kernel(m_ref, b_ref, kept_ref, green_ref, up_ref, down_ref):
    @pl.when(place()[0] == 2)
    def _():
        @pl.loop(0, 2)
        def _(i):
            halves_to(dot_t(b_ref[...], kept_ref[i]), down_ref, i)
            halves_to(dot_t(green_ref[i], m_ref[...]), up_ref, i)


def cross(m, b, kept, far_b):
    rows = m.shape[0]
    return pl.pallas_call(
        cross_kernel,
        out_shape=(jax.ShapeDtypeStruct((2, 2, rows, rows // 2), BF16),) * 2,
        in_specs=[VMEM] * 4,
        out_specs=(VMEM,) * 2,
        compiler_params=pltpu.CompilerParams(vmem_limit_bytes=12 * MIB),
        cost_estimate=cost(8 * rows * rows * 3072, 5 * rows * 3072 * 2),
        name="cross",
    )(m, b, kept, far_b)


def select_kernel(own_ref, m1_ref, m2_ref, t1_ref, t2_ref, up_ref, down_ref, *refs):
    outs, all_ref = refs[:-1], refs[-1]
    p, odd = place()
    me = lax.axis_index("orb")

    def put(used, at, x_ref):
        @pl.when(used)
        def _():
            q = jnp.where(odd == 1, 3 - at, at)
            for h in range(2):
                all_ref[(q * 2 + h) ^ me] = x_ref[h]

    put(p >= 0, p, own_ref)
    put(p >= 1, p - 1, m1_ref)
    put(p >= 2, p - 2, m2_ref)
    put(p <= 2, p + 1, t1_ref)
    put(p <= 1, p + 2, t2_ref)
    put(p == 3, 0, up_ref)
    put(p == 0, 3, down_ref)
    for k, out_ref in enumerate(outs):
        out_ref[...] = all_ref[k]


def select(parts):
    shape = (2,) + parts[0].shape[2:]
    return pl.pallas_call(
        select_kernel,
        out_shape=(jax.ShapeDtypeStruct(shape, BF16),) * 8,
        in_specs=[VMEM] * len(parts),
        out_specs=(VMEM,) * 8,
        scratch_shapes=[pltpu.VMEM((8,) + shape, BF16)],
        compiler_params=pltpu.CompilerParams(vmem_limit_bytes=12 * MIB),
        cost_estimate=cost(1e5, 16 * parts[0].size),
        name="select",
    )(*parts)


def total_kernel(per, *refs):
    x0, x1, out_ref = refs[:8], refs[8:16], refs[16]
    _, rows, width = x0[0].shape
    me = lax.axis_index("orb")
    r, q = lax.axis_index("ri"), me // 2
    straight = []
    for other in range(2):
        odd = (me + other) % 2
        p, t = jnp.where(odd == 1, 3 - r, r), jnp.where(odd == 1, 3 - q, q)
        straight.append(t <= p)
    blocks = width // per
    lane = iota((per, width), 1) // per
    for o in range(rows // per):
        at = slice(o * per, (o + 1) * per)

        def sums(xs, i, at=at):
            x = xs[0][i, at].astype(F32)
            for x_ref in xs[1:]:
                x = x + x_ref[i, at].astype(F32)
            return x

        quads = {(0, 0): sums(x0, 0), (1, 1): sums(x1, 1)}
        low, high = 0.0, 0.0
        for other in range(2):
            a, b = sums(x0[other::2], 1), sums(x1[other::2], 0)
            low = low + jnp.where(straight[other], a, b)
            high = high + jnp.where(straight[other], b, a)
        quads[1, 0], quads[0, 1] = low, high
        for i in range(2):
            for tile in range(2):
                moved = None
                for b in range(blocks):
                    came = blocks // 2 * tile + b // 2
                    shift = ((b - came) * per) % width
                    x = quads[i, b % 2]
                    x = pltpu.roll(x, shift, 1) if shift else x
                    moved = x if moved is None else jnp.where(lane == b, x, moved)
                to = (o * 2 + i) * per
                out_ref[to : to + per, tile * width : (tile + 1) * width] = moved


def total(per, parts):
    _, rows, width = parts[0].shape
    return pl.pallas_call(
        functools.partial(total_kernel, per),
        out_shape=jax.ShapeDtypeStruct((2 * rows, 2 * width), F32),
        in_specs=[VMEM] * len(parts),
        out_specs=VMEM,
        compiler_params=pltpu.CompilerParams(vmem_limit_bytes=12 * MIB),
        cost_estimate=cost(1e7, 4 * parts[0].size),
        name="total",
    )(*parts)


def local(planes, orbs, integrals, screen, green_occ, green_virt):
    rows, groups, _ = integrals.shape
    per = rows // CHUNKS

    def send(x, pairs):
        flat = []
        for orb in range(orbs):
            for source, target in pairs:
                if orb % 2:
                    source, target = planes - 1 - source, planes - 1 - target
                flat.append((source * orbs + orb, target * orbs + orb))
        return lax.ppermute(x, ("ri", "orb"), flat)

    def swap(x):
        return lax.all_to_all(x, "orb", split_axis=0, concat_axis=0, tiled=True)

    x = integrals.reshape(rows * groups, 3072)
    screen = screen.reshape(-1)
    w1, w2 = weights(green_occ, green_virt)

    def xors(pieces):
        out = [pieces[0]]
        for k in range(1, orbs):
            pairs = [(q * orbs + i, q * orbs + (i ^ k)) for q in range(planes) for i in range(orbs)]
            out.append(lax.ppermute(pieces[k], ("ri", "orb"), pairs))
        return out

    (m,) = prep(0, x, screen, groups, per, False)
    ms = [swap(m).reshape(orbs * per, 3072)]
    pieces = prep(1, x, screen, groups, per, True)
    pieces, halves = pieces[:orbs], pieces[orbs:]
    pieces = xors(pieces)
    ms.append(assemble(pieces))
    b, kept = green(ms, w1, w2, False)
    even = lax.ppermute(halves[0], "ri", [(0, 1), (1, 2), (2, 3)])
    odd = lax.ppermute(halves[1], "ri", [(3, 2), (2, 1), (1, 0)])
    pieces = unpack(even, odd)
    pieces = xors(pieces)
    hopped = assemble(pieces)

    mine, theirs, b_of, got = {}, {}, {}, {}
    for c in range(CHUNKS):
        got["f1", c] = send(ms[c], [(0, 1), (1, 2), (2, 3)]) if c == 0 else hopped
        got["f2", c] = send(got["f1", c], [(1, 2), (2, 3)])
        got["g", c] = send(ms[c], [(3, 2)])
        for kind in USERS:
            mine[kind, c], theirs[kind, c], *b_of[kind, c] = pair(kind, got[kind, c], w1, w2, kept, b)
    far_b, far_kept = green([got["g", c] for c in range(CHUNKS)], w1, w2, True)
    sums = []
    for c in range(CHUNKS):
        own_block = own(b, kept, c)
        up, down = cross(got["f2", c], b_of["f2", c][0], far_kept, far_b)
        back = [
            send(theirs["f1", c], [(1, 0), (2, 1), (3, 2)]),
            send(theirs["f2", c], [(2, 0), (3, 1)]),
            send(up, [(2, 3)]),
            send(down, [(2, 0)]),
        ]
        pieces = select([own_block] + [mine[kind, c] for kind in USERS] + back)
        sums += xors(pieces)
    return total(per, sums)


def padded_2(block, sides, width):
    for axis, dim in sides:
        count = lax.axis_size(axis)
        forward = [(i, i + 1) for i in range(count - 1)]
        backward = [(target, source) for source, target in forward]
        low = lax.ppermute(
            lax.slice_in_dim(block, block.shape[dim] - width, None, axis=dim), axis, forward
        )
        high = lax.ppermute(lax.slice_in_dim(block, 0, width, axis=dim), axis, backward)
        block = jnp.concatenate([low, block, high], axis=dim)
    return block


def green_apply(extended, green_occ, green_ext):
    groups = green_occ.shape[0]
    rows = extended.shape[0]
    basis = green_occ.shape[-1]
    shaped = extended.reshape(rows, groups + 2, basis, 3, basis)
    total = None
    for t in range(3):
        slab = shaped[:, t : t + groups]
        padded = jnp.pad(slab, ((0, 0), (0, 0), (0, 0), (1, 1), (0, 0)))
        window = padded[:, :, :, 2 - t : 5 - t]
        term = jnp.einsum(
            "gnm,pgmsl->pgnsl", green_occ[:, t], window, preferred_element_type=jnp.float32
        )
        total = term if total is None else total + term
    occ_side = total.astype(jnp.bfloat16)
    chosen = jnp.stack([green_ext[s : s + groups] for s in range(3)], axis=1)
    both = jnp.einsum("pgnsl,gsla->pgnsa", occ_side, chosen, preferred_element_type=jnp.float32)
    return both.astype(jnp.bfloat16).reshape(rows, groups, -1)


def local_any(integrals, screen, green_occ, green_virt):
    rows = integrals.shape[0]
    groups = integrals.shape[1]
    basis = green_occ.shape[-1]
    blocks = jnp.repeat(screen, RB, axis=2)
    target = jnp.arange(groups)[:, None] + jnp.arange(3)[None, :] - 1
    inside = ((target >= 0) & (target < groups)).astype(jnp.int32)
    keep = jnp.transpose(blocks * inside[:, :, None], (2, 0, 1)).astype(jnp.bfloat16)
    shaped = integrals.reshape(rows, groups, basis, 3, basis)
    masked = (shaped * keep[:, :, None, :, None]).reshape(rows, groups, -1)
    green_ext = jnp.pad(green_virt, ((1, 1), (0, 0), (0, 0)))
    masked_mine = lax.all_to_all(masked, "orb", split_axis=1, concat_axis=0, tiled=True)
    local_groups = masked_mine.shape[1]
    first = lax.axis_index("orb") * local_groups
    extended = padded_2(masked_mine, (("orb", 1),), 1)
    occ_mine = lax.dynamic_slice_in_dim(green_occ, first, local_groups, 0)
    virt_mine = lax.dynamic_slice_in_dim(green_ext, first, local_groups + 2, 0)
    both_mine = green_apply(extended, occ_mine, virt_mine)
    left = both_mine.reshape(both_mine.shape[0], -1)
    piece = lax.all_gather(masked_mine, "ri", axis=0, tiled=True)
    right = piece.reshape(piece.shape[0], -1)
    partial_chi = lax.dot_general(
        left, right, (((1,), (1,)), ((), ())), preferred_element_type=jnp.float32
    )
    return lax.psum_scatter(partial_chi, "orb", scatter_dimension=1, tiled=True)


def solution(mesh):
    planes, orbs = mesh.shape["ri"], mesh.shape["orb"]
    placed = (P(("ri", "orb"), None, None), P(None, None, ("ri", "orb")), P(), P())

    if planes != 4 or orbs != 8:
        return jax.shard_map(local_any, mesh=mesh, in_specs=placed, out_specs=P("ri", "orb"), check_vma=False)

    def body(*args):
        return local(planes, orbs, *args)

    return jax.shard_map(body, mesh=mesh, in_specs=placed, out_specs=P("ri", "orb"), check_vma=False)
```

```python
import functools

import jax
import jax.numpy as jnp
from jax import lax
from jax.experimental import pallas as pl
from jax.experimental.pallas import tpu as pltpu
from jax.sharding import PartitionSpec as P

RB = 16
CHUNKS = 2
BF16 = jnp.bfloat16
F32 = jnp.float32
VMEM = pl.BlockSpec(memory_space=pltpu.VMEM)
SMEM = pl.BlockSpec(memory_space=pltpu.SMEM)
MIB = 1024 * 1024


def iota(shape, dim):
    return lax.broadcasted_iota(jnp.int32, shape, dim)


def dot(x, y):
    return lax.dot_general(x, y, (((1,), (0,)), ((), ())), preferred_element_type=F32)


def dot_t(x, y):
    return lax.dot_general(x, y, (((1,), (1,)), ((), ())), preferred_element_type=F32)


def ones_where(test):
    return jnp.where(test, 1.0, 0.0).astype(BF16)


def cost(flops, moved):
    return pl.CostEstimate(flops=int(flops), bytes_accessed=int(moved), transcendentals=0)


def prep_kernel(groups, blocks, c, per, apart, screen_ref, x_ref, *refs):
    *outs, lanes_ref = refs

    def kept(d):
        return outs[d % 2].at[d // 2] if apart else outs[0].at[d]

    rows, first = per * groups, c * (per // RB)
    lane, row = iota((1536, 128), 1), iota((1536, 128), 0)
    base = row - (lane // 8) * 96 - lane % 8
    for g in range(12):
        lanes_ref[:, g * 128 : (g + 1) * 128] = ones_where(base == g * 8)
    to, of = iota((rows, rows), 0), iota((rows, rows), 1)
    by_group = ones_where(of == (to % per) * groups + to // per)
    for h in range(2):
        x = dot(by_group, x_ref[:, h * 1536 : (h + 1) * 1536]).astype(BF16)
        for s in range(3):
            y = dot(x, lanes_ref[:, s * 512 : (s + 1) * 512])
            for a in range(groups):
                d = a + s - 1
                if not 0 <= d < groups:
                    continue
                for b in range(per // RB):
                    keep = screen_ref[(a * 3 + s) * blocks + first + b].astype(F32)
                    at = a * per + b * RB
                    z = (y[at : at + RB] * keep).astype(BF16)
                    for j in range(4):
                        col = (2 - s) * 1024 + j * 256 + h * 128
                        kept(d)[b * RB : (b + 1) * RB, col : col + 128] = z[:, j * 128 : (j + 1) * 128]
    zeros = jnp.zeros((per, 1024), BF16)
    kept(0)[:, :1024] = zeros
    kept(groups - 1)[:, 2048:] = zeros


def prep(c, x, screen, groups, per, apart):
    blocks = screen.shape[0] // (groups * 3)
    rows = per * groups
    shapes = [jax.ShapeDtypeStruct((groups, per, 3072), BF16)]
    if apart:
        shapes = [jax.ShapeDtypeStruct((groups // 2, per, 3072), BF16)] * 2
    return pl.pallas_call(
        functools.partial(prep_kernel, groups, blocks, c, per, apart),
        out_shape=shapes,
        in_specs=[SMEM, VMEM],
        out_specs=[VMEM] * len(shapes),
        scratch_shapes=[pltpu.VMEM((1536, 1536), BF16)],
        compiler_params=pltpu.CompilerParams(vmem_limit_bytes=24 * MIB),
        cost_estimate=cost(4 * rows * 1536 * 1536, rows * 3072 * 4),
    )(screen, x[c * rows : (c + 1) * rows])


def unpack_kernel(even_ref, odd_ref, *outs):
    me = lax.axis_index("orb")
    for k, out_ref in enumerate(outs):
        to = me ^ k
        for odd, x_ref in enumerate((even_ref, odd_ref)):

            @pl.when(to % 2 == odd)
            def _(x_ref=x_ref, out_ref=out_ref, to=to):
                out_ref[...] = x_ref[to // 2]


def unpack(even, odd):
    return pl.pallas_call(
        unpack_kernel,
        out_shape=[jax.ShapeDtypeStruct(even.shape[1:], BF16)] * 8,
        in_specs=[VMEM] * 2,
        out_specs=[VMEM] * 8,
        compiler_params=pltpu.CompilerParams(vmem_limit_bytes=12 * MIB),
        cost_estimate=cost(1e5, 8 * even.size),
        name="unpack",
    )(even, odd)


def assemble_kernel(*refs):
    out_ref = refs[-1]
    per = refs[0].shape[0]
    me = lax.axis_index("orb")
    for k, x_ref in enumerate(refs[:-1]):
        out_ref[pl.ds(pl.multiple_of((me ^ k) * per, per), per)] = x_ref[...]


def assemble(pieces):
    per, width = pieces[0].shape
    return pl.pallas_call(
        assemble_kernel,
        out_shape=jax.ShapeDtypeStruct((8 * per, width), BF16),
        in_specs=[VMEM] * 8,
        out_specs=VMEM,
        compiler_params=pltpu.CompilerParams(vmem_limit_bytes=12 * MIB),
        cost_estimate=cost(1e5, 32 * per * width),
        name="assemble",
    )(*pieces)


def weights_kernel(occ_ref, virt_ref, w1_ref, w2_ref):
    d = lax.axis_index("orb")
    last = occ_ref.shape[0] - 1
    spread = ones_where(iota((256, 32), 0) // 8 == iota((256, 32), 1))
    same = iota((256, 256), 0) % 8 == iota((256, 256), 1) % 8
    for c in range(3):
        at = jnp.clip(d + (c - 1), 0, last)
        for a in range(3):
            t = a - c + 1
            if 0 <= t <= 2:
                half = dot_t(spread, occ_ref[at, t]).astype(BF16)
                block = jnp.where(same, dot_t(half, spread), 0.0)
            else:
                block = jnp.zeros((256, 256), F32)
            w1_ref[a * 256 : (a + 1) * 256, c * 256 : (c + 1) * 256] = block.astype(BF16)
    row = iota((512, 32), 0)
    spread = ones_where((row // 128) * 8 + row % 8 == iota((512, 32), 1))
    same = (iota((512, 512), 0) % 128) // 8 == (iota((512, 512), 1) % 128) // 8
    half = dot(spread, virt_ref[d]).astype(BF16)
    w2_ref[...] = jnp.where(same, dot_t(half, spread), 0.0).astype(BF16)


def weights(occ, virt):
    return pl.pallas_call(
        weights_kernel,
        out_shape=(jax.ShapeDtypeStruct((768, 768), BF16), jax.ShapeDtypeStruct((512, 512), BF16)),
        in_specs=[VMEM, VMEM],
        out_specs=(VMEM, VMEM),
        compiler_params=pltpu.CompilerParams(vmem_limit_bytes=12 * MIB),
        cost_estimate=cost(1e8, 2e6),
        name="weights",
    )(occ, virt)


def apply_green(m_ref, w1_ref, w2_ref, y_ref, out_ref):
    for j in range(4):
        for c in range(3):
            lo, hi = max(c - 1, 0), min(c + 1, 2) + 1
            x = jnp.concatenate([m_ref[:, a * 1024 + j * 256 : a * 1024 + (j + 1) * 256] for a in range(lo, hi)], axis=1)
            y = dot(x, w1_ref[lo * 256 : hi * 256, c * 256 : (c + 1) * 256])
            y_ref[:, j * 768 + c * 256 : j * 768 + (c + 1) * 256] = y.astype(BF16)
    for c in range(3):
        for h in range(2):
            at = c * 256 + h * 128
            x = jnp.concatenate([y_ref[:, j * 768 + at : j * 768 + at + 128] for j in range(4)], axis=1)
            z = dot(x, w2_ref[...]).astype(BF16)
            for j in range(4):
                col = c * 1024 + j * 256 + h * 128
                out_ref[:, col : col + 128] = z[:, j * 128 : (j + 1) * 128]


def green_kernel(far, m0_ref, m1_ref, w1_ref, w2_ref, out_ref, kept_ref, y_ref):
    def run():
        kept_ref[0] = m0_ref[...]
        kept_ref[1] = m1_ref[...]

        @pl.loop(0, 2)
        def _(c):
            apply_green(kept_ref.at[c], w1_ref, w2_ref, y_ref, out_ref.at[c])

    if far:
        pl.when(place()[0] == 2)(run)
    else:
        run()


def green(ms, w1, w2, far):
    rows = ms[0].shape[0]
    return pl.pallas_call(
        functools.partial(green_kernel, far),
        out_shape=(jax.ShapeDtypeStruct((2, rows, 3072), BF16),) * 2,
        in_specs=[VMEM] * 4,
        out_specs=(VMEM,) * 2,
        scratch_shapes=[pltpu.VMEM((rows, 3072), BF16)],
        compiler_params=pltpu.CompilerParams(vmem_limit_bytes=12 * MIB),
        cost_estimate=cost(rows * 14e6, rows * 3072 * 12),
        name="green",
    )(*ms, w1, w2)


def halves_to(x, out_ref, i):
    width = out_ref.shape[3]
    for h in range(2):
        out_ref[h, i] = x[:, h * width : (h + 1) * width].astype(BF16)


def own_kernel(c, b_ref, m_ref, out_ref):
    @pl.loop(0, 2)
    def _(i):
        halves_to(dot_t(b_ref[i], m_ref[c]), out_ref, i)


def own(b, m, c):
    rows = m.shape[1]
    return pl.pallas_call(
        functools.partial(own_kernel, c),
        out_shape=jax.ShapeDtypeStruct((2, 2, rows, rows // 2), BF16),
        in_specs=[VMEM] * 2,
        out_specs=VMEM,
        compiler_params=pltpu.CompilerParams(vmem_limit_bytes=12 * MIB),
        cost_estimate=cost(4 * rows * rows * 3072, 3 * rows * 3072 * 2),
        name="own",
    )(b, m)


USERS = {"f1": (1, 3), "f2": (2, 3)}


def place():
    r, odd = lax.axis_index("ri"), lax.axis_index("orb") % 2
    return jnp.where(odd == 1, 3 - r, r), odd


def pair_kernel(kind, m_ref, w1_ref, w2_ref, kept_ref, green_ref, mine_ref, theirs_ref, b_ref, y_ref):
    p, _ = place()
    first, last = USERS[kind]

    @pl.when((p >= first) & (p <= last))
    def _():
        apply_green(m_ref, w1_ref, w2_ref, y_ref, b_ref)

        @pl.loop(0, 2)
        def _(i):
            halves_to(dot_t(b_ref[...], kept_ref[i]), theirs_ref, i)
            halves_to(dot_t(green_ref[i], m_ref[...]), mine_ref, i)


def pair(kind, m, w1, w2, kept, b):
    rows = m.shape[0]
    keep = kind == "f2"
    block = jax.ShapeDtypeStruct((2, 2, rows, rows // 2), BF16)
    return pl.pallas_call(
        functools.partial(pair_kernel, kind),
        out_shape=(block, block) + (jax.ShapeDtypeStruct(m.shape, BF16),) * keep,
        in_specs=[VMEM] * 5,
        out_specs=(VMEM,) * (2 + keep),
        scratch_shapes=[pltpu.VMEM((rows, 3072), BF16)] * (2 - keep),
        compiler_params=pltpu.CompilerParams(vmem_limit_bytes=12 * MIB),
        cost_estimate=cost(rows * 7e6 + 8 * rows * rows * 3072, 5 * rows * 3072 * 2),
    )(m, w1, w2, kept, b)


def cross_kernel(m_ref, b_ref, kept_ref, green_ref, up_ref, down_ref):
    @pl.when(place()[0] == 2)
    def _():
        @pl.loop(0, 2)
        def _(i):
            halves_to(dot_t(b_ref[...], kept_ref[i]), down_ref, i)
            halves_to(dot_t(green_ref[i], m_ref[...]), up_ref, i)


def cross(m, b, kept, far_b):
    rows = m.shape[0]
    return pl.pallas_call(
        cross_kernel,
        out_shape=(jax.ShapeDtypeStruct((2, 2, rows, rows // 2), BF16),) * 2,
        in_specs=[VMEM] * 4,
        out_specs=(VMEM,) * 2,
        compiler_params=pltpu.CompilerParams(vmem_limit_bytes=12 * MIB),
        cost_estimate=cost(8 * rows * rows * 3072, 5 * rows * 3072 * 2),
        name="cross",
    )(m, b, kept, far_b)


def select_kernel(own_ref, m1_ref, m2_ref, t1_ref, t2_ref, up_ref, down_ref, *refs):
    outs, all_ref = refs[:-1], refs[-1]
    p, odd = place()
    me = lax.axis_index("orb")

    def put(used, at, x_ref):
        @pl.when(used)
        def _():
            q = jnp.where(odd == 1, 3 - at, at)
            for h in range(2):
                all_ref[(q * 2 + h) ^ me] = x_ref[h]

    put(p >= 0, p, own_ref)
    put(p >= 1, p - 1, m1_ref)
    put(p >= 2, p - 2, m2_ref)
    put(p <= 2, p + 1, t1_ref)
    put(p <= 1, p + 2, t2_ref)
    put(p == 3, 0, up_ref)
    put(p == 0, 3, down_ref)
    for k, out_ref in enumerate(outs):
        out_ref[...] = all_ref[k]


def select(parts):
    shape = (2,) + parts[0].shape[2:]
    return pl.pallas_call(
        select_kernel,
        out_shape=(jax.ShapeDtypeStruct(shape, BF16),) * 8,
        in_specs=[VMEM] * len(parts),
        out_specs=(VMEM,) * 8,
        scratch_shapes=[pltpu.VMEM((8,) + shape, BF16)],
        compiler_params=pltpu.CompilerParams(vmem_limit_bytes=12 * MIB),
        cost_estimate=cost(1e5, 16 * parts[0].size),
        name="select",
    )(*parts)


def total_kernel(per, *refs):
    x0, x1, out_ref = refs[:8], refs[8:16], refs[16]
    _, rows, width = x0[0].shape
    me = lax.axis_index("orb")
    r, q = lax.axis_index("ri"), me // 2
    straight = []
    for other in range(2):
        odd = (me + other) % 2
        p, t = jnp.where(odd == 1, 3 - r, r), jnp.where(odd == 1, 3 - q, q)
        straight.append(t <= p)
    blocks = width // per
    lane = iota((per, width), 1) // per
    for o in range(rows // per):
        at = slice(o * per, (o + 1) * per)

        def sums(xs, i, at=at):
            x = xs[0][i, at].astype(F32)
            for x_ref in xs[1:]:
                x = x + x_ref[i, at].astype(F32)
            return x

        quads = {(0, 0): sums(x0, 0), (1, 1): sums(x1, 1)}
        low, high = 0.0, 0.0
        for other in range(2):
            a, b = sums(x0[other::2], 1), sums(x1[other::2], 0)
            low = low + jnp.where(straight[other], a, b)
            high = high + jnp.where(straight[other], b, a)
        quads[1, 0], quads[0, 1] = low, high
        for i in range(2):
            for tile in range(2):
                moved = None
                for b in range(blocks):
                    came = blocks // 2 * tile + b // 2
                    shift = ((b - came) * per) % width
                    x = quads[i, b % 2]
                    x = pltpu.roll(x, shift, 1) if shift else x
                    moved = x if moved is None else jnp.where(lane == b, x, moved)
                to = (o * 2 + i) * per
                out_ref[to : to + per, tile * width : (tile + 1) * width] = moved


def total(per, parts):
    _, rows, width = parts[0].shape
    return pl.pallas_call(
        functools.partial(total_kernel, per),
        out_shape=jax.ShapeDtypeStruct((2 * rows, 2 * width), F32),
        in_specs=[VMEM] * len(parts),
        out_specs=VMEM,
        compiler_params=pltpu.CompilerParams(vmem_limit_bytes=12 * MIB),
        cost_estimate=cost(1e7, 4 * parts[0].size),
        name="total",
    )(*parts)


def local(planes, orbs, integrals, screen, green_occ, green_virt):
    rows, groups, _ = integrals.shape
    per = rows // CHUNKS

    def send(x, pairs):
        flat = []
        for orb in range(orbs):
            for source, target in pairs:
                if orb % 2:
                    source, target = planes - 1 - source, planes - 1 - target
                flat.append((source * orbs + orb, target * orbs + orb))
        return lax.ppermute(x, ("ri", "orb"), flat)

    def swap(x):
        return lax.all_to_all(x, "orb", split_axis=0, concat_axis=0, tiled=True)

    x = integrals.reshape(rows * groups, 3072)
    screen = screen.reshape(-1)
    w1, w2 = weights(green_occ, green_virt)

    def xors(pieces):
        out = [pieces[0]]
        for k in range(1, orbs):
            pairs = [(q * orbs + i, q * orbs + (i ^ k)) for q in range(planes) for i in range(orbs)]
            out.append(lax.ppermute(pieces[k], ("ri", "orb"), pairs))
        return out

    (m,) = prep(0, x, screen, groups, per, False)
    x, m = lax.optimization_barrier((x, m))
    ms = [swap(m).reshape(orbs * per, 3072)]
    halves = prep(1, x, screen, groups, per, True)
    pieces = unpack(*halves)
    pieces = xors(pieces)
    ms.append(assemble(pieces))
    b, kept = green(ms, w1, w2, False)
    even = lax.ppermute(halves[0], "ri", [(0, 1), (1, 2), (2, 3)])
    odd = lax.ppermute(halves[1], "ri", [(3, 2), (2, 1), (1, 0)])
    pieces = unpack(even, odd)
    pieces = xors(pieces)
    hopped = assemble(pieces)

    mine, theirs, b_of, got = {}, {}, {}, {}
    for c in range(CHUNKS):
        got["f1", c] = send(ms[c], [(0, 1), (1, 2), (2, 3)]) if c == 0 else hopped
        got["f2", c] = send(got["f1", c], [(1, 2), (2, 3)])
        got["g", c] = send(ms[c], [(3, 2)])
        for kind in USERS:
            mine[kind, c], theirs[kind, c], *b_of[kind, c] = pair(kind, got[kind, c], w1, w2, kept, b)
    far_b, far_kept = green([got["g", c] for c in range(CHUNKS)], w1, w2, True)
    sums = []
    for c in range(CHUNKS):
        own_block = own(b, kept, c)
        up, down = cross(got["f2", c], b_of["f2", c][0], far_kept, far_b)
        back = [
            send(theirs["f1", c], [(1, 0), (2, 1), (3, 2)]),
            send(theirs["f2", c], [(2, 0), (3, 1)]),
            send(up, [(2, 3)]),
            send(down, [(2, 0)]),
        ]
        pieces = select([own_block] + [mine[kind, c] for kind in USERS] + back)
        sums += xors(pieces)
    return total(per, sums)


def padded_2(block, sides, width):
    for axis, dim in sides:
        count = lax.axis_size(axis)
        forward = [(i, i + 1) for i in range(count - 1)]
        backward = [(target, source) for source, target in forward]
        low = lax.ppermute(
            lax.slice_in_dim(block, block.shape[dim] - width, None, axis=dim), axis, forward
        )
        high = lax.ppermute(lax.slice_in_dim(block, 0, width, axis=dim), axis, backward)
        block = jnp.concatenate([low, block, high], axis=dim)
    return block


def green_apply(extended, green_occ, green_ext):
    groups = green_occ.shape[0]
    rows = extended.shape[0]
    basis = green_occ.shape[-1]
    shaped = extended.reshape(rows, groups + 2, basis, 3, basis)
    total = None
    for t in range(3):
        slab = shaped[:, t : t + groups]
        padded = jnp.pad(slab, ((0, 0), (0, 0), (0, 0), (1, 1), (0, 0)))
        window = padded[:, :, :, 2 - t : 5 - t]
        term = jnp.einsum(
            "gnm,pgmsl->pgnsl", green_occ[:, t], window, preferred_element_type=jnp.float32
        )
        total = term if total is None else total + term
    occ_side = total.astype(jnp.bfloat16)
    chosen = jnp.stack([green_ext[s : s + groups] for s in range(3)], axis=1)
    both = jnp.einsum("pgnsl,gsla->pgnsa", occ_side, chosen, preferred_element_type=jnp.float32)
    return both.astype(jnp.bfloat16).reshape(rows, groups, -1)


def local_any(integrals, screen, green_occ, green_virt):
    rows = integrals.shape[0]
    groups = integrals.shape[1]
    basis = green_occ.shape[-1]
    blocks = jnp.repeat(screen, RB, axis=2)
    target = jnp.arange(groups)[:, None] + jnp.arange(3)[None, :] - 1
    inside = ((target >= 0) & (target < groups)).astype(jnp.int32)
    keep = jnp.transpose(blocks * inside[:, :, None], (2, 0, 1)).astype(jnp.bfloat16)
    shaped = integrals.reshape(rows, groups, basis, 3, basis)
    masked = (shaped * keep[:, :, None, :, None]).reshape(rows, groups, -1)
    green_ext = jnp.pad(green_virt, ((1, 1), (0, 0), (0, 0)))
    masked_mine = lax.all_to_all(masked, "orb", split_axis=1, concat_axis=0, tiled=True)
    local_groups = masked_mine.shape[1]
    first = lax.axis_index("orb") * local_groups
    extended = padded_2(masked_mine, (("orb", 1),), 1)
    occ_mine = lax.dynamic_slice_in_dim(green_occ, first, local_groups, 0)
    virt_mine = lax.dynamic_slice_in_dim(green_ext, first, local_groups + 2, 0)
    both_mine = green_apply(extended, occ_mine, virt_mine)
    left = both_mine.reshape(both_mine.shape[0], -1)
    piece = lax.all_gather(masked_mine, "ri", axis=0, tiled=True)
    right = piece.reshape(piece.shape[0], -1)
    partial_chi = lax.dot_general(
        left, right, (((1,), (1,)), ((), ())), preferred_element_type=jnp.float32
    )
    return lax.psum_scatter(partial_chi, "orb", scatter_dimension=1, tiled=True)


def solution(mesh):
    planes, orbs = mesh.shape["ri"], mesh.shape["orb"]
    placed = (P(("ri", "orb"), None, None), P(None, None, ("ri", "orb")), P(), P())

    if planes != 4 or orbs != 8:
        return jax.shard_map(local_any, mesh=mesh, in_specs=placed, out_specs=P("ri", "orb"), check_vma=False)

    def body(*args):
        return local(planes, orbs, *args)

    return jax.shard_map(body, mesh=mesh, in_specs=placed, out_specs=P("ri", "orb"), check_vma=False)
```

```python
import functools

import jax
import jax.numpy as jnp
from jax import lax
from jax.experimental import pallas as pl
from jax.experimental.pallas import tpu as pltpu
from jax.sharding import PartitionSpec as P

RB = 16
CHUNKS = 2
BF16 = jnp.bfloat16
F32 = jnp.float32
VMEM = pl.BlockSpec(memory_space=pltpu.VMEM)
SMEM = pl.BlockSpec(memory_space=pltpu.SMEM)
MIB = 1024 * 1024


def iota(shape, dim):
    return lax.broadcasted_iota(jnp.int32, shape, dim)


def dot(x, y):
    return lax.dot_general(x, y, (((1,), (0,)), ((), ())), preferred_element_type=F32)


def dot_t(x, y):
    return lax.dot_general(x, y, (((1,), (1,)), ((), ())), preferred_element_type=F32)


def ones_where(test):
    return jnp.where(test, 1.0, 0.0).astype(BF16)


def cost(flops, moved):
    return pl.CostEstimate(flops=int(flops), bytes_accessed=int(moved), transcendentals=0)


def prep_kernel(groups, blocks, c, per, apart, screen_ref, x_ref, *refs):
    *outs, lanes_ref = refs

    def kept(d):
        return outs[d % 2].at[d // 2] if apart else outs[0].at[d]

    rows, first = per * groups, c * (per // RB)
    lane, row = iota((1536, 128), 1), iota((1536, 128), 0)
    base = row - (lane // 8) * 96 - lane % 8
    for g in range(12):
        lanes_ref[:, g * 128 : (g + 1) * 128] = ones_where(base == g * 8)
    to, of = iota((rows, rows), 0), iota((rows, rows), 1)
    by_group = ones_where(of == (to % per) * groups + to // per)
    for h in range(2):
        x = dot(by_group, x_ref[:, h * 1536 : (h + 1) * 1536]).astype(BF16)
        for s in range(3):
            y = dot(x, lanes_ref[:, s * 512 : (s + 1) * 512])
            for a in range(groups):
                d = a + s - 1
                if not 0 <= d < groups:
                    continue
                for b in range(per // RB):
                    keep = screen_ref[(a * 3 + s) * blocks + first + b].astype(F32)
                    at = a * per + b * RB
                    z = (y[at : at + RB] * keep).astype(BF16)
                    for j in range(4):
                        col = (2 - s) * 1024 + j * 256 + h * 128
                        kept(d)[b * RB : (b + 1) * RB, col : col + 128] = z[:, j * 128 : (j + 1) * 128]
    zeros = jnp.zeros((per, 1024), BF16)
    kept(0)[:, :1024] = zeros
    kept(groups - 1)[:, 2048:] = zeros


def prep(c, x, screen, groups, per, apart):
    blocks = screen.shape[0] // (groups * 3)
    rows = per * groups
    shapes = [jax.ShapeDtypeStruct((groups, per, 3072), BF16)]
    if apart:
        shapes = [jax.ShapeDtypeStruct((groups // 2, per, 3072), BF16)] * 2
    return pl.pallas_call(
        functools.partial(prep_kernel, groups, blocks, c, per, apart),
        out_shape=shapes,
        in_specs=[SMEM, VMEM],
        out_specs=[VMEM] * len(shapes),
        scratch_shapes=[pltpu.VMEM((1536, 1536), BF16)],
        compiler_params=pltpu.CompilerParams(vmem_limit_bytes=24 * MIB),
        cost_estimate=cost(4 * rows * 1536 * 1536, rows * 3072 * 4),
    )(screen, x[c * rows : (c + 1) * rows])


def unpack_kernel(even_ref, odd_ref, *outs):
    me = lax.axis_index("orb")
    for k, out_ref in enumerate(outs):
        to = me ^ k
        for odd, x_ref in enumerate((even_ref, odd_ref)):

            @pl.when(to % 2 == odd)
            def _(x_ref=x_ref, out_ref=out_ref, to=to):
                out_ref[...] = x_ref[to // 2]


def unpack(even, odd):
    return pl.pallas_call(
        unpack_kernel,
        out_shape=[jax.ShapeDtypeStruct(even.shape[1:], BF16)] * 8,
        in_specs=[VMEM] * 2,
        out_specs=[VMEM] * 8,
        compiler_params=pltpu.CompilerParams(vmem_limit_bytes=12 * MIB),
        cost_estimate=cost(1e5, 8 * even.size),
        name="unpack",
    )(even, odd)


def assemble_kernel(*refs):
    out_ref = refs[-1]
    per = refs[0].shape[0]
    me = lax.axis_index("orb")
    for k, x_ref in enumerate(refs[:-1]):
        out_ref[pl.ds(pl.multiple_of((me ^ k) * per, per), per)] = x_ref[...]


def assemble(pieces):
    per, width = pieces[0].shape
    return pl.pallas_call(
        assemble_kernel,
        out_shape=jax.ShapeDtypeStruct((8 * per, width), BF16),
        in_specs=[VMEM] * 8,
        out_specs=VMEM,
        compiler_params=pltpu.CompilerParams(vmem_limit_bytes=12 * MIB),
        cost_estimate=cost(1e5, 32 * per * width),
        name="assemble",
    )(*pieces)


def weights_kernel(occ_ref, virt_ref, w1_ref, w2_ref):
    d = lax.axis_index("orb")
    last = occ_ref.shape[0] - 1
    spread = ones_where(iota((256, 32), 0) // 8 == iota((256, 32), 1))
    same = iota((256, 256), 0) % 8 == iota((256, 256), 1) % 8
    for c in range(3):
        at = jnp.clip(d + (c - 1), 0, last)
        for a in range(3):
            t = a - c + 1
            if 0 <= t <= 2:
                half = dot_t(spread, occ_ref[at, t]).astype(BF16)
                block = jnp.where(same, dot_t(half, spread), 0.0)
            else:
                block = jnp.zeros((256, 256), F32)
            w1_ref[a * 256 : (a + 1) * 256, c * 256 : (c + 1) * 256] = block.astype(BF16)
    row = iota((512, 32), 0)
    spread = ones_where((row // 128) * 8 + row % 8 == iota((512, 32), 1))
    same = (iota((512, 512), 0) % 128) // 8 == (iota((512, 512), 1) % 128) // 8
    half = dot(spread, virt_ref[d]).astype(BF16)
    w2_ref[...] = jnp.where(same, dot_t(half, spread), 0.0).astype(BF16)


def weights(occ, virt):
    return pl.pallas_call(
        weights_kernel,
        out_shape=(jax.ShapeDtypeStruct((768, 768), BF16), jax.ShapeDtypeStruct((512, 512), BF16)),
        in_specs=[VMEM, VMEM],
        out_specs=(VMEM, VMEM),
        compiler_params=pltpu.CompilerParams(vmem_limit_bytes=12 * MIB),
        cost_estimate=cost(1e8, 2e6),
        name="weights",
    )(occ, virt)


def apply_green(m_ref, w1_ref, w2_ref, y_ref, out_ref):
    for j in range(4):
        for c in range(3):
            lo, hi = max(c - 1, 0), min(c + 1, 2) + 1
            x = jnp.concatenate([m_ref[:, a * 1024 + j * 256 : a * 1024 + (j + 1) * 256] for a in range(lo, hi)], axis=1)
            y = dot(x, w1_ref[lo * 256 : hi * 256, c * 256 : (c + 1) * 256])
            y_ref[:, j * 768 + c * 256 : j * 768 + (c + 1) * 256] = y.astype(BF16)
    for c in range(3):
        for h in range(2):
            at = c * 256 + h * 128
            x = jnp.concatenate([y_ref[:, j * 768 + at : j * 768 + at + 128] for j in range(4)], axis=1)
            z = dot(x, w2_ref[...]).astype(BF16)
            for j in range(4):
                col = c * 1024 + j * 256 + h * 128
                out_ref[:, col : col + 128] = z[:, j * 128 : (j + 1) * 128]


def green_kernel(m0_ref, m1_ref, w1_ref, w2_ref, out_ref, kept_ref, y_ref):
    kept_ref[0] = m0_ref[...]
    kept_ref[1] = m1_ref[...]

    @pl.loop(0, 2)
    def _(c):
        apply_green(kept_ref.at[c], w1_ref, w2_ref, y_ref, out_ref.at[c])


def far_kernel(m_ref, w1_ref, w2_ref, out_ref, y_ref):
    @pl.when(place()[0] == 2)
    def _():
        apply_green(m_ref, w1_ref, w2_ref, y_ref, out_ref)


def far_green(m, w1, w2):
    return pl.pallas_call(
        far_kernel,
        out_shape=jax.ShapeDtypeStruct(m.shape, BF16),
        in_specs=[VMEM] * 3,
        out_specs=VMEM,
        scratch_shapes=[pltpu.VMEM(m.shape, BF16)],
        compiler_params=pltpu.CompilerParams(vmem_limit_bytes=12 * MIB),
        cost_estimate=cost(m.shape[0] * 7e6, m.size * 4),
        name="far_green",
    )(m, w1, w2)


def green(ms, w1, w2):
    rows = ms[0].shape[0]
    return pl.pallas_call(
        green_kernel,
        out_shape=(jax.ShapeDtypeStruct((2, rows, 3072), BF16),) * 2,
        in_specs=[VMEM] * 4,
        out_specs=(VMEM,) * 2,
        scratch_shapes=[pltpu.VMEM((rows, 3072), BF16)],
        compiler_params=pltpu.CompilerParams(vmem_limit_bytes=12 * MIB),
        cost_estimate=cost(rows * 14e6, rows * 3072 * 12),
        name="green",
    )(*ms, w1, w2)


def halves_to(x, out_ref, i):
    width = out_ref.shape[3]
    for h in range(2):
        out_ref[h, i] = x[:, h * width : (h + 1) * width].astype(BF16)


def own_kernel(c, b_ref, m_ref, out_ref):
    @pl.loop(0, 2)
    def _(i):
        halves_to(dot_t(b_ref[i], m_ref[c]), out_ref, i)


def own(b, m, c):
    rows = m.shape[1]
    return pl.pallas_call(
        functools.partial(own_kernel, c),
        out_shape=jax.ShapeDtypeStruct((2, 2, rows, rows // 2), BF16),
        in_specs=[VMEM] * 2,
        out_specs=VMEM,
        compiler_params=pltpu.CompilerParams(vmem_limit_bytes=12 * MIB),
        cost_estimate=cost(4 * rows * rows * 3072, 3 * rows * 3072 * 2),
        name="own",
    )(b, m)


USERS = {"f1": (1, 3), "f2": (2, 3)}


def place():
    r, odd = lax.axis_index("ri"), lax.axis_index("orb") % 2
    return jnp.where(odd == 1, 3 - r, r), odd


def pair_kernel(kind, m_ref, w1_ref, w2_ref, kept_ref, green_ref, mine_ref, theirs_ref, b_ref, y_ref):
    p, _ = place()
    first, last = USERS[kind]

    @pl.when((p >= first) & (p <= last))
    def _():
        apply_green(m_ref, w1_ref, w2_ref, y_ref, b_ref)

        @pl.loop(0, 2)
        def _(i):
            halves_to(dot_t(b_ref[...], kept_ref[i]), theirs_ref, i)
            halves_to(dot_t(green_ref[i], m_ref[...]), mine_ref, i)


def pair(kind, m, w1, w2, kept, b):
    rows = m.shape[0]
    keep = kind == "f2"
    block = jax.ShapeDtypeStruct((2, 2, rows, rows // 2), BF16)
    return pl.pallas_call(
        functools.partial(pair_kernel, kind),
        out_shape=(block, block) + (jax.ShapeDtypeStruct(m.shape, BF16),) * keep,
        in_specs=[VMEM] * 5,
        out_specs=(VMEM,) * (2 + keep),
        scratch_shapes=[pltpu.VMEM((rows, 3072), BF16)] * (2 - keep),
        compiler_params=pltpu.CompilerParams(vmem_limit_bytes=12 * MIB),
        cost_estimate=cost(rows * 7e6 + 8 * rows * rows * 3072, 5 * rows * 3072 * 2),
    )(m, w1, w2, kept, b)


def cross_kernel(m_ref, b_ref, m0_ref, m1_ref, b0_ref, b1_ref, up_ref, down_ref):
    @pl.when(place()[0] == 2)
    def _():
        for i, (far_m_ref, far_b_ref) in enumerate(((m0_ref, b0_ref), (m1_ref, b1_ref))):
            halves_to(dot_t(b_ref[...], far_m_ref[...]), down_ref, i)
            halves_to(dot_t(far_b_ref[...], m_ref[...]), up_ref, i)


def cross(m, b, far_m, far_b):
    rows = m.shape[0]
    return pl.pallas_call(
        cross_kernel,
        out_shape=(jax.ShapeDtypeStruct((2, 2, rows, rows // 2), BF16),) * 2,
        in_specs=[VMEM] * 6,
        out_specs=(VMEM,) * 2,
        compiler_params=pltpu.CompilerParams(vmem_limit_bytes=12 * MIB),
        cost_estimate=cost(8 * rows * rows * 3072, 5 * rows * 3072 * 2),
        name="cross",
    )(m, b, *far_m, *far_b)


def select_kernel(own_ref, m1_ref, m2_ref, t1_ref, t2_ref, up_ref, down_ref, *refs):
    outs, all_ref = refs[:-1], refs[-1]
    p, odd = place()
    me = lax.axis_index("orb")

    def put(used, at, x_ref):
        @pl.when(used)
        def _():
            q = jnp.where(odd == 1, 3 - at, at)
            for h in range(2):
                all_ref[(q * 2 + h) ^ me] = x_ref[h]

    put(p >= 0, p, own_ref)
    put(p >= 1, p - 1, m1_ref)
    put(p >= 2, p - 2, m2_ref)
    put(p <= 2, p + 1, t1_ref)
    put(p <= 1, p + 2, t2_ref)
    put(p == 3, 0, up_ref)
    put(p == 0, 3, down_ref)
    for k, out_ref in enumerate(outs):
        out_ref[...] = all_ref[k]


def select(parts):
    shape = (2,) + parts[0].shape[2:]
    return pl.pallas_call(
        select_kernel,
        out_shape=(jax.ShapeDtypeStruct(shape, BF16),) * 8,
        in_specs=[VMEM] * len(parts),
        out_specs=(VMEM,) * 8,
        scratch_shapes=[pltpu.VMEM((8,) + shape, BF16)],
        compiler_params=pltpu.CompilerParams(vmem_limit_bytes=12 * MIB),
        cost_estimate=cost(1e5, 16 * parts[0].size),
        name="select",
    )(*parts)


def total_kernel(per, *refs):
    x0, x1, out_ref = refs[:8], refs[8:16], refs[16]
    _, rows, width = x0[0].shape
    me = lax.axis_index("orb")
    r, q = lax.axis_index("ri"), me // 2
    straight = []
    for other in range(2):
        odd = (me + other) % 2
        p, t = jnp.where(odd == 1, 3 - r, r), jnp.where(odd == 1, 3 - q, q)
        straight.append(t <= p)
    blocks = width // per
    lane = iota((per, width), 1) // per
    for o in range(rows // per):
        at = slice(o * per, (o + 1) * per)

        def sums(xs, i, at=at):
            x = xs[0][i, at].astype(F32)
            for x_ref in xs[1:]:
                x = x + x_ref[i, at].astype(F32)
            return x

        quads = {(0, 0): sums(x0, 0), (1, 1): sums(x1, 1)}
        low, high = 0.0, 0.0
        for other in range(2):
            a, b = sums(x0[other::2], 1), sums(x1[other::2], 0)
            low = low + jnp.where(straight[other], a, b)
            high = high + jnp.where(straight[other], b, a)
        quads[1, 0], quads[0, 1] = low, high
        for i in range(2):
            for tile in range(2):
                moved = None
                for b in range(blocks):
                    came = blocks // 2 * tile + b // 2
                    shift = ((b - came) * per) % width
                    x = quads[i, b % 2]
                    x = pltpu.roll(x, shift, 1) if shift else x
                    moved = x if moved is None else jnp.where(lane == b, x, moved)
                to = (o * 2 + i) * per
                out_ref[to : to + per, tile * width : (tile + 1) * width] = moved


def total(per, parts):
    _, rows, width = parts[0].shape
    return pl.pallas_call(
        functools.partial(total_kernel, per),
        out_shape=jax.ShapeDtypeStruct((2 * rows, 2 * width), F32),
        in_specs=[VMEM] * len(parts),
        out_specs=VMEM,
        compiler_params=pltpu.CompilerParams(vmem_limit_bytes=12 * MIB),
        cost_estimate=cost(1e7, 4 * parts[0].size),
        name="total",
    )(*parts)


def local(planes, orbs, integrals, screen, green_occ, green_virt):
    rows, groups, _ = integrals.shape
    per = rows // CHUNKS

    def send(x, pairs):
        flat = []
        for orb in range(orbs):
            for source, target in pairs:
                if orb % 2:
                    source, target = planes - 1 - source, planes - 1 - target
                flat.append((source * orbs + orb, target * orbs + orb))
        return lax.ppermute(x, ("ri", "orb"), flat)

    def swap(x):
        return lax.all_to_all(x, "orb", split_axis=0, concat_axis=0, tiled=True)

    x = integrals.reshape(rows * groups, 3072)
    screen = screen.reshape(-1)
    w1, w2 = weights(green_occ, green_virt)

    def xors(pieces):
        out = [pieces[0]]
        for k in range(1, orbs):
            pairs = [(q * orbs + i, q * orbs + (i ^ k)) for q in range(planes) for i in range(orbs)]
            out.append(lax.ppermute(pieces[k], ("ri", "orb"), pairs))
        return out

    (m,) = prep(0, x, screen, groups, per, False)
    x, m = lax.optimization_barrier((x, m))
    ms = [swap(m).reshape(orbs * per, 3072)]
    halves = prep(1, x, screen, groups, per, True)
    pieces = unpack(*halves)
    pieces = xors(pieces)
    ms.append(assemble(pieces))
    b, kept = green(ms, w1, w2)
    even = lax.ppermute(halves[0], "ri", [(0, 1), (1, 2), (2, 3)])
    odd = lax.ppermute(halves[1], "ri", [(3, 2), (2, 1), (1, 0)])
    pieces = unpack(even, odd)
    pieces = xors(pieces)
    hopped = assemble(pieces)

    mine, theirs, b_of, got = {}, {}, {}, {}
    for c in range(CHUNKS):
        got["f1", c] = send(ms[c], [(0, 1), (1, 2), (2, 3)]) if c == 0 else hopped
        got["f2", c] = send(got["f1", c], [(1, 2), (2, 3)])
        got["g", c] = send(ms[c], [(3, 2)])
        for kind in USERS:
            mine[kind, c], theirs[kind, c], *b_of[kind, c] = pair(kind, got[kind, c], w1, w2, kept, b)
    far_m, far_b = [got["g", c] for c in range(CHUNKS)], []
    for c in range(CHUNKS):
        far_b.append(far_green(far_m[c], w1, w2))
    sums = []
    for c in range(CHUNKS):
        own_block = own(b, kept, c)
        up, down = cross(got["f2", c], b_of["f2", c][0], far_m, far_b)
        back = [
            send(theirs["f1", c], [(1, 0), (2, 1), (3, 2)]),
            send(theirs["f2", c], [(2, 0), (3, 1)]),
            send(up, [(2, 3)]),
            send(down, [(2, 0)]),
        ]
        pieces = select([own_block] + [mine[kind, c] for kind in USERS] + back)
        sums += xors(pieces)
    return total(per, sums)


def padded_2(block, sides, width):
    for axis, dim in sides:
        count = lax.axis_size(axis)
        forward = [(i, i + 1) for i in range(count - 1)]
        backward = [(target, source) for source, target in forward]
        low = lax.ppermute(
            lax.slice_in_dim(block, block.shape[dim] - width, None, axis=dim), axis, forward
        )
        high = lax.ppermute(lax.slice_in_dim(block, 0, width, axis=dim), axis, backward)
        block = jnp.concatenate([low, block, high], axis=dim)
    return block


def green_apply(extended, green_occ, green_ext):
    groups = green_occ.shape[0]
    rows = extended.shape[0]
    basis = green_occ.shape[-1]
    shaped = extended.reshape(rows, groups + 2, basis, 3, basis)
    total = None
    for t in range(3):
        slab = shaped[:, t : t + groups]
        padded = jnp.pad(slab, ((0, 0), (0, 0), (0, 0), (1, 1), (0, 0)))
        window = padded[:, :, :, 2 - t : 5 - t]
        term = jnp.einsum(
            "gnm,pgmsl->pgnsl", green_occ[:, t], window, preferred_element_type=jnp.float32
        )
        total = term if total is None else total + term
    occ_side = total.astype(jnp.bfloat16)
    chosen = jnp.stack([green_ext[s : s + groups] for s in range(3)], axis=1)
    both = jnp.einsum("pgnsl,gsla->pgnsa", occ_side, chosen, preferred_element_type=jnp.float32)
    return both.astype(jnp.bfloat16).reshape(rows, groups, -1)


def local_any(integrals, screen, green_occ, green_virt):
    rows = integrals.shape[0]
    groups = integrals.shape[1]
    basis = green_occ.shape[-1]
    blocks = jnp.repeat(screen, RB, axis=2)
    target = jnp.arange(groups)[:, None] + jnp.arange(3)[None, :] - 1
    inside = ((target >= 0) & (target < groups)).astype(jnp.int32)
    keep = jnp.transpose(blocks * inside[:, :, None], (2, 0, 1)).astype(jnp.bfloat16)
    shaped = integrals.reshape(rows, groups, basis, 3, basis)
    masked = (shaped * keep[:, :, None, :, None]).reshape(rows, groups, -1)
    green_ext = jnp.pad(green_virt, ((1, 1), (0, 0), (0, 0)))
    masked_mine = lax.all_to_all(masked, "orb", split_axis=1, concat_axis=0, tiled=True)
    local_groups = masked_mine.shape[1]
    first = lax.axis_index("orb") * local_groups
    extended = padded_2(masked_mine, (("orb", 1),), 1)
    occ_mine = lax.dynamic_slice_in_dim(green_occ, first, local_groups, 0)
    virt_mine = lax.dynamic_slice_in_dim(green_ext, first, local_groups + 2, 0)
    both_mine = green_apply(extended, occ_mine, virt_mine)
    left = both_mine.reshape(both_mine.shape[0], -1)
    piece = lax.all_gather(masked_mine, "ri", axis=0, tiled=True)
    right = piece.reshape(piece.shape[0], -1)
    partial_chi = lax.dot_general(
        left, right, (((1,), (1,)), ((), ())), preferred_element_type=jnp.float32
    )
    return lax.psum_scatter(partial_chi, "orb", scatter_dimension=1, tiled=True)


def solution(mesh):
    planes, orbs = mesh.shape["ri"], mesh.shape["orb"]
    placed = (P(("ri", "orb"), None, None), P(None, None, ("ri", "orb")), P(), P())

    if planes != 4 or orbs != 8:
        return jax.shard_map(local_any, mesh=mesh, in_specs=placed, out_specs=P("ri", "orb"), check_vma=False)

    def body(*args):
        return local(planes, orbs, *args)

    return jax.shard_map(body, mesh=mesh, in_specs=placed, out_specs=P("ri", "orb"), check_vma=False)
```
